512 devices in a mesh: dp: 64 (over x, z), expert: 8 (over y, core).
Axes of the slice: x: 4, y: 4, z: 16, core: 2. Of those that a mesh axis runs over, the one named last changes fastest.
Arguments:
- tokens: bfloat16 [8192, 2048], P('dp'), may hold values from -6 to 6
- arms: int32 [8192], P('dp'), may hold values from 0 to 3
- arm_bias: bfloat16 [4, 2048], replicated, may hold values from -3 to 3
- routes: int32 [8192, 6], P('dp'), may hold values from 0 to 63, all different within a row; in each aligned block of 128 rows (0 to 127, 128 to 255, ...) at most 16 rows name the same one
- gates: int32 [8192, 6], P('dp'), may hold values from 1 to 64
- up_weight: bfloat16 [64, 1408, 2048], P('dp', 'expert'), may hold values from -0.125 to 0.125
- down_weight: bfloat16 [64, 1408, 2048], P('dp', 'expert'), may hold values from -0.15625 to 0.15625
- cotangent: bfloat16 [8192, 2048], P('dp'), may hold values from -1.5 to 1.5
Outputs:
- grad_tokens: float32 [8192, 2048], P('dp', 'expert')
- grad_up: bfloat16 [64, 1408, 2048], P('dp', 'expert')
- grad_down: bfloat16 [64, 1408, 2048], P('dp', 'expert')
The draws below stay inside these ranges and needn't reach their ends.
Inputs may be any that keep to these rules, and one draw needn't show every extreme that they name: The 6 ids of a token differ. Among the routes of the 128 tokens of one index of dp, at most 16 name one expert, and in some such block some expert is named exactly 16 times.
All inputs are finite; a program needn't handle non-finite values.
Results may differ from the reference program's by a relative error of at most 0.014.
Values may be sent and summed in bfloat16 or wider, within the bound.
A program may use at most 128 MiB of HBM per device.

```python
import math
import jax
import jax.numpy as jnp
import numpy as np
from jax import lax

D = 2048
H = 1408
EXPERTS = 64
TOPK = 6
ARMS = 4
TOK_DEV = 128
CAP = 16
HS = 176
TOKENS = 8192
N_DP = 64
N_EXPERT = 8


def set_ends(result, key, low, largest):
    shape = result.shape
    index_at = [jax.random.randint(jax.random.fold_in(key, axis), (), 0, shape[axis]) for axis in range(len(shape))]
    result = result.at[tuple(index_at)].set(low)
    longest = shape.index(max(shape))
    index_at[longest] = (index_at[longest] + 1) % shape[longest]
    return result.at[tuple(index_at)].set(largest)


def block_scale(own_key, extent, pieces, smallest, largest):
    level, own = 1.0, jax.random.fold_in(own_key, 6)
    for position, blocks in pieces:
        draws = jnp.exp(jax.random.uniform(jax.random.fold_in(own, position), (blocks,), jnp.float32, smallest / len(pieces), largest / len(pieces)))
        level = level * jnp.repeat(draws, extent[position] // blocks).reshape([-1 if axis == position else 1 for axis in range(len(extent))])
    return level


def shared_out(own_key, own, number, rows, count, top, most, skew):
    order = jax.random.permutation(own_key, count)
    packed, common = portions_of(count, rows * top, most, skew, True), portions_of(count, rows * top, most, skew, False)
    places = jnp.arange(count)

    def named(lengths, offset_by):
        used = int((lengths > 0).sum())
        fixed = max(1, used // 4)
        moved = fixed + (places - fixed + offset_by * (used - fixed)) % max(1, count - fixed)
        return jnp.zeros((count,), jnp.int32).at[order[jnp.where(places < fixed, places, moved)]].set(jnp.asarray(lengths, jnp.int32))

    lengths = jnp.where(number % 4 == 0, named(packed, number // 4), named(common, number - number // 4 - 1))
    mixed = jax.random.permutation(jax.random.fold_in(own, 3), count)
    donor, receiver = mixed[0:count // 2 * 2:2], mixed[1:count // 2 * 2:2]
    room = jnp.minimum(lengths[donor] - 1, most - lengths[receiver]) // 2
    room = jnp.where((donor == order[0]) | (receiver == order[0]) | (lengths[receiver] == 0), 0, jnp.maximum(room, 0))
    moved = jax.random.randint(jax.random.fold_in(own, 4), (count // 2,), 0, 1 << 20) % (room + 1)
    lengths = lengths.at[donor].add(-moved).at[receiver].add(moved)
    labels = jnp.searchsorted(jnp.cumsum(lengths), jnp.arange(rows * top), side="right").astype(jnp.int32)
    grid = labels.reshape(top, rows).T
    grid = grid[jax.random.permutation(jax.random.fold_in(own, 1), rows)]
    offset_by = jax.random.randint(jax.random.fold_in(own, 2), (rows, 1), 0, top)
    return jnp.take_along_axis(grid, (jnp.arange(top)[None, :] + offset_by) % top, axis=1)


def portions_of(amount, total, bound, slope, full):
    portions = [(1 << 20) // math.isqrt(standing ** slope) + 1 for standing in range(1, amount + 1)]
    largest = bound if full else min(bound, max(-(-total // amount), total * portions[0] // sum(portions)))
    least = 1 if total - largest >= amount - 1 else 0
    given, rest = [largest] + [least] * (amount - 1), total - largest - least * (amount - 1)
    while rest > 0:
        movable = [i for i in range(1, amount) if given[i] < largest] or [i for i in range(1, amount) if given[i] < bound]
        whole, remaining = sum([portions[i] for i in movable]), rest
        for i in movable:
            extra = min(bound - given[i], max(1, remaining * portions[i] // whole), rest)
            given[i] = given[i] + extra
            rest = rest - extra
    return np.array(given)


def gaussian(key, shape, scale, reach, pieces=(), kind=jnp.bfloat16):
    result = scale * jax.random.normal(key, shape, jnp.float32)
    if pieces:
        result = result * block_scale(key, shape, pieces, -0.22, 0.18)
    return jnp.clip(result, -reach, reach).astype(kind)


def setup_inputs(seed: int = 0) -> dict:
    streams_of = jax.random.split(jax.random.key(seed), 9)
    tokens = gaussian(streams_of[0], (TOKENS, D), 1.0, 6.0, ((0, 64),))
    arms = set_ends(jax.random.randint(streams_of[1], (TOKENS,), 0, ARMS), jax.random.fold_in(streams_of[1], 1), 0, ARMS - 1).astype(jnp.int32)
    arm_bias = gaussian(streams_of[2], (ARMS, D), 0.5, 3.0)
    routes_keys = jax.random.split(jax.random.fold_in(streams_of[3], 1), TOKENS // TOK_DEV)
    routes_turns = jax.random.permutation(jax.random.fold_in(streams_of[3], 3), TOKENS // TOK_DEV)
    routes = jax.vmap(lambda own, number: shared_out(jax.random.fold_in(streams_of[3], 2), own, number, TOK_DEV, EXPERTS, TOPK, CAP, 2))(routes_keys, routes_turns).reshape((TOKENS, TOPK))
    gates = set_ends(jax.random.randint(streams_of[4], (TOKENS, TOPK), 1, 65), jax.random.fold_in(streams_of[4], 1), 1, 64).astype(jnp.int32)
    up_weight = gaussian(streams_of[5], (EXPERTS, H, D), D ** -0.5, 0.125, ((0, 64), (1, 8)))
    down_weight = gaussian(streams_of[6], (EXPERTS, H, D), H ** -0.5, 0.15625, ((0, 64), (1, 8)))
    cotangent = gaussian(streams_of[7], (TOKENS, D), 0.25, 1.5, ((0, 64),))
    return dict(tokens=tokens, arms=arms, arm_bias=arm_bias, routes=routes, gates=gates, up_weight=up_weight, down_weight=down_weight, cotangent=cotangent)


def slot_table(routes):
    flat_ids = routes.reshape(N_DP, TOK_DEV * TOPK).astype(jnp.int32)
    expert_ids = jnp.arange(EXPERTS, dtype=jnp.int32)
    one_hot = (flat_ids[:, :, None] == expert_ids[None, None, :]).astype(jnp.int32)
    rank_table = jnp.cumsum(one_hot, axis=1) - one_hot
    slot_ids = jnp.sum(rank_table * one_hot, axis=2)
    return slot_ids.reshape(-1).astype(jnp.int32)


def reference(tokens, arms, arm_bias, routes, gates, up_weight, down_weight, cotangent):
    lifted = (tokens.astype(jnp.float32) + arm_bias.astype(jnp.float32)[arms]).astype(jnp.bfloat16)
    route_count = TOKENS * TOPK
    flat_routes = routes.reshape(-1).astype(jnp.int32)
    slot_ids = slot_table(routes)
    positions = jnp.arange(route_count, dtype=jnp.int32)
    owner_block = positions // (TOK_DEV * TOPK)
    target_pos = flat_routes * (N_DP * CAP) + owner_block * CAP + slot_ids
    index_table = jnp.full((EXPERTS * N_DP * CAP,), -1, jnp.int32).at[target_pos].set(positions)
    index_table = index_table.reshape(EXPERTS, N_DP * CAP)
    route_weight = gates.reshape(-1).astype(jnp.float32) / 64.0

    def one_expert(running_sum, expert_item):
        row_index, w_up, w_down = expert_item
        live_mask = row_index >= 0
        safe_index = jnp.maximum(row_index, 0)
        token_index = safe_index // TOPK
        expert_rows = jnp.where(live_mask[:, None], lifted[token_index], jnp.zeros((), jnp.bfloat16))
        slot_weight = jnp.where(live_mask, route_weight[safe_index], jnp.zeros((), jnp.float32))
        scaled = (cotangent[token_index].astype(jnp.float32) * slot_weight[:, None]).astype(jnp.bfloat16)
        preact = jnp.dot(expert_rows, w_up.T, preferred_element_type=jnp.float32)
        hidden = jax.nn.silu(preact).astype(jnp.bfloat16)
        backprop = jnp.dot(scaled, w_down.T, preferred_element_type=jnp.float32)
        sigmoid_pre = jax.nn.sigmoid(preact)
        grad_pre = (backprop * sigmoid_pre * (1.0 + preact * (1.0 - sigmoid_pre))).astype(jnp.bfloat16)
        expert_down = jnp.dot(hidden.T, scaled, preferred_element_type=jnp.float32).astype(jnp.bfloat16)
        expert_up = jnp.dot(grad_pre.T, expert_rows, preferred_element_type=jnp.float32).astype(jnp.bfloat16)
        block_terms = jnp.einsum("rsu,sud->rsd", grad_pre.astype(jnp.float32).reshape(-1, N_EXPERT, HS),
                                 w_up.astype(jnp.float32).reshape(N_EXPERT, HS, D)).astype(jnp.bfloat16)
        contrib = jnp.sum(block_terms.astype(jnp.float32), axis=1)
        contrib = jnp.where(live_mask[:, None], contrib, jnp.zeros((), jnp.float32))
        running_sum = running_sum.at[token_index].add(contrib)
        return running_sum, (expert_up, expert_down)

    start_sum = jnp.zeros((TOKENS, D), jnp.float32)
    grad_tokens, (grad_up, grad_down) = lax.scan(one_expert, start_sum, (index_table, up_weight, down_weight))
    return (grad_tokens, grad_up, grad_down)
```

```python
import jax
import jax.numpy as jnp
from jax import lax
from jax.sharding import PartitionSpec as P

EXPERTS = 64
TOPK = 6
CAP = 16


def local(tokens, arms, arm_bias, routes, gates, up_weight, down_weight, cotangent):
    token_count, width = tokens.shape
    hidden_local = up_weight.shape[1]
    expert_ways = lax.axis_size("expert")
    part = width // expert_ways
    offset = lax.axis_index("expert") * part
    f32, bf16 = jnp.float32, jnp.bfloat16
    own = lambda a: lax.dynamic_slice_in_dim(a, offset, part, axis=1)
    arm_pick = (arms[:, None] == jnp.arange(arm_bias.shape[0])[None, :]).astype(bf16)
    lifted = (
        own(tokens).astype(f32) + jnp.dot(arm_pick, own(arm_bias), preferred_element_type=f32)
    ).astype(bf16)
    hits = routes[:, :, None] == jnp.arange(EXPERTS, dtype=jnp.int32)
    member = jnp.any(hits, axis=1)
    gate_of = jnp.sum(jnp.where(hits, gates[:, :, None], 0), axis=1)
    earlier = jnp.tri(token_count, k=-1, dtype=bf16)
    rank = jnp.dot(earlier, member.astype(bf16), preferred_element_type=f32).astype(jnp.int32)
    slot = jnp.where(member, rank, -1)
    place = slot.T[:, None, :] == jnp.arange(CAP, dtype=jnp.int32)[None, :, None]
    place = place.reshape(EXPERTS * CAP, token_count)
    weight = jnp.where(
        place, jnp.repeat(gate_of.T.astype(f32) / 64.0, CAP, axis=0), 0.0
    ).astype(bf16)
    place = place.astype(bf16)
    rows = jnp.concatenate(
        [
            jnp.dot(place, lifted, preferred_element_type=f32).astype(bf16),
            jnp.dot(weight, own(cotangent), preferred_element_type=f32).astype(bf16),
        ],
        axis=1,
    )
    arrived = lax.all_to_all(
        rows.reshape(EXPERTS, CAP, 2 * part), "dp", split_axis=0, concat_axis=0, tiled=True
    ).reshape(EXPERTS * CAP, 2 * part)
    everything = lax.all_gather(arrived, "expert", axis=0, tiled=False)
    up = up_weight[0]
    down = down_weight[0]
    x = jnp.concatenate([everything[i, :, :part] for i in range(expert_ways)], axis=1)
    s = jnp.concatenate([everything[i, :, part:] for i in range(expert_ways)], axis=1)
    preact = jnp.einsum("rd,hd->rh", x, up, preferred_element_type=f32)
    backprop = jnp.einsum("rd,hd->rh", s, down, preferred_element_type=f32)
    sigmoid_pre = jax.nn.sigmoid(preact)
    hidden = (preact * sigmoid_pre).astype(bf16)
    grad_pre = (backprop * sigmoid_pre * (1.0 + preact * (1.0 - sigmoid_pre))).astype(bf16)
    partial_value = jnp.einsum("rh,hd->rd", grad_pre, up, preferred_element_type=f32).astype(bf16)
    grad_down = jnp.einsum("rh,rd->hd", hidden, s, preferred_element_type=f32).astype(bf16)
    grad_up = jnp.einsum("rh,rd->hd", grad_pre, x, preferred_element_type=f32).astype(bf16)
    summed = lax.psum_scatter(partial_value, "expert", scatter_dimension=1, tiled=True)
    returned = lax.all_to_all(
        summed.reshape(EXPERTS, CAP, part), "dp", split_axis=0, concat_axis=0, tiled=True
    ).reshape(EXPERTS * CAP, part)
    grad_tokens = lax.dot_general(
        place, returned, (((0,), (0,)), ((), ())), preferred_element_type=f32
    )
    return grad_tokens, grad_up[None], grad_down[None]


def solution(mesh):
    in_specs = (
        P("dp", None),
        P("dp"),
        P(),
        P("dp", None),
        P("dp", None),
        P("dp", "expert", None),
        P("dp", "expert", None),
        P("dp", None),
    )
    out_specs = (P("dp", "expert"), P("dp", "expert", None), P("dp", "expert", None))
    return jax.shard_map(local, mesh=mesh, in_specs=in_specs, out_specs=out_specs, check_vma=False)
```

```python
import jax
import jax.numpy as jnp
from jax import lax
from jax.experimental import pallas as pl
from jax.experimental.pallas import tpu as pltpu
from jax.sharding import PartitionSpec as P

MESH = pl.DeviceIdType.MESH
F32, BF16 = jnp.float32, jnp.bfloat16

TOK = 128
CAP = 16
PART = 256
HID = 176
HPAD = 256
NX, NY, NZ = 4, 4, 16
META = 16
TOPK = 6
UNITS = 8
GROUPS = 4
ROWS = 1024
WIDTH = 2048


def place_rows(slot, gate, first):
    index = lax.broadcasted_iota(jnp.int32, (CAP, TOK), 0).astype(F32)
    hot, weighted = [], []
    for i in range(NX):
        here = jnp.broadcast_to(slot[first + i : first + i + 1], (CAP, TOK)) == index
        hot.append(jnp.where(here, 1.0, 0.0))
        if gate is not None:
            weight = jnp.broadcast_to(gate[first + i : first + i + 1], (CAP, TOK))
            weighted.append(jnp.where(here, weight, 0.0))
    hot = jnp.concatenate(hot, axis=0)
    return hot, (jnp.concatenate(weighted, axis=0) if weighted else None)


def slots_of(meta, ids, earlier):
    hits = jnp.zeros(ids.shape, F32)
    gate = jnp.zeros(ids.shape, F32)
    for k in range(TOPK):
        same = jnp.broadcast_to(meta[k : k + 1, :TOK], ids.shape) == ids
        hits = hits + jnp.where(same, 1.0, 0.0)
        gate = gate + jnp.where(same, jnp.broadcast_to(meta[k : k + 1, TOK:], ids.shape), 0.0)
    rank = jnp.dot(hits.astype(BF16), earlier, preferred_element_type=F32)
    return jnp.where(hits > 0.5, rank, -1.0), gate


def kernel(
    tokens, arms, bias, meta_in, up_in, down_in, cot,
    gtok_out, gup_out, gdown_out,
    tok, zbuf, xs, rows, up, down, hid_t, gpre_t, pall, pr, q, fb, db, cs, cr, ts, u_buf, v_buf,
    gup, gdown, gtok, tri, own_hot,
    in_sem, out_sem, zs, zr, xsem, xrem, y1s, y1r, y2s, y2r, cos, cor, rps, rpr, rys, ryr, rxs, rxr, rzs, rzr,
):
    dp, ex = lax.axis_index("dp"), lax.axis_index("expert")
    x, z = dp // NZ, lax.rem(dp, NZ)
    y, core = ex // 2, lax.rem(ex, 2)
    xz = lambda dx, dz: lax.rem(x + dx + NX, NX) * NZ + lax.rem(z + dz + NZ, NZ)
    yof = lambda dy: lax.rem(y + dy + NY, NY)
    exof = lambda dy: yof(dy) * 2 + core
    partner = y * 2 + (1 - core)

    def remote(src, dst, send, recv, to):
        return pltpu.make_async_remote_copy(
            src_ref=src, dst_ref=dst, send_sem=send, recv_sem=recv, device_id=to, device_id_type=MESH
        )

    barrier = pltpu.get_barrier_semaphore()
    peers = [(xz(d, 0), ex) for d in (1, 2, 3)]
    peers += [(dp, exof(1)), (dp, exof(-1)), (dp, partner)]
    for to in peers:
        pl.semaphore_signal(barrier, inc=1, device_id=to, device_id_type=MESH)

    @pl.loop(1, NZ)
    def _(d):
        pl.semaphore_signal(barrier, inc=1, device_id=(xz(0, d), ex), device_id_type=MESH)

    lanes = pl.ds(pl.multiple_of(ex * PART, PART), PART)
    load_tok = pltpu.make_async_copy(tokens.at[:, lanes], tok, in_sem.at[0])
    load_cot = pltpu.make_async_copy(cot.at[:, lanes], zbuf.at[0, pl.ds(TOK + META, TOK)], in_sem.at[1])
    load_meta = pltpu.make_async_copy(meta_in, zbuf.at[0, pl.ds(TOK, META)], in_sem.at[2])
    load_up = pltpu.make_async_copy(up_in, up.at[pl.ds(0, HID)], in_sem.at[3])
    load_down = pltpu.make_async_copy(down_in, down.at[pl.ds(0, HID)], in_sem.at[4])
    for load in (load_tok, load_meta, load_cot, load_up, load_down):
        load.start()
    arm_row = jnp.broadcast_to(arms[...], (TOK, TOK))
    arm_hot = jnp.where(arm_row == lax.broadcasted_iota(jnp.int32, (TOK, TOK), 0), 1.0, 0.0).T
    own_bias = bias[:, lanes].astype(F32)
    added = jnp.zeros((TOK, PART), F32)
    for a in range(own_bias.shape[0]):
        added = added + arm_hot[:, a : a + 1] * own_bias[a : a + 1]
    tri[...] = jnp.where(
        lax.broadcasted_iota(jnp.int32, (TOK, TOK), 0) < lax.broadcasted_iota(jnp.int32, (TOK, TOK), 1), 1.0, 0.0
    ).astype(BF16)
    load_tok.wait()
    zbuf[0, pl.ds(0, TOK)] = (tok[...].astype(F32) + added).astype(BF16)
    load_meta.wait()
    load_cot.wait()
    pl.semaphore_wait(barrier, len(peers) + NZ - 1)

    pieces = ((0, TOK + META), (TOK + META, TOK))

    def z_copy(to_slot, from_slot, step, piece):
        at = pl.ds(*pieces[piece])
        return remote(
            zbuf.at[from_slot, at], zbuf.at[to_slot, at], zs.at[to_slot, piece], zr.at[to_slot, piece], (xz(0, step), ex)
        )

    for piece in (0, 1):
        z_copy(1, 0, 1, piece).start()
        z_copy(2, 0, -1, piece).start()

    x_copy = lambda u, dx: remote(
        xs.at[dx - 1, pl.ds(2 * u, 2)], rows.at[ex, pl.ds(2 * u, 2), dx],
        xsem.at[u, dx - 1], xrem.at[u, dx - 1], (xz(dx, 0), ex),
    )
    y1_copy = lambda u, k: remote(
        rows.at[ex, pl.ds(2 * u, 2)], rows.at[ex, pl.ds(2 * u, 2)],
        y1s.at[u, k], y1r.at[u, k], (dp, exof(1 - 2 * k)),
    )

    def y2_copy(u, k):
        part = rows.at[exof(2 * k - 1), pl.ds(2 * u, 2), pl.ds(2 * k, 2)]
        return remote(part, part, y2s.at[u, k], y2r.at[u, k], (dp, exof(1 - 2 * k)))

    def core_copy(u, k):
        part = rows.at[exof((0, -1, 1, 2)[k]), pl.ds(2 * u, 2)]
        return remote(part, part, cos.at[u, k], cor.at[u, k], (dp, partner))

    up[pl.ds(HID, HPAD - HID)] = jnp.zeros((HPAD - HID, WIDTH), BF16)
    down[pl.ds(HID, HPAD - HID)] = jnp.zeros((HPAD - HID, WIDTH), BF16)

    def arrive(u):
        @pl.when(u >= 1)
        def _():
            for piece in (0, 1):
                z_copy(2 * u, 0, -1, piece).wait_recv()

                @pl.when(u < UNITS - 1)
                def _():
                    z_copy(2 * u + 2, 2 * u, -1, piece).start()

        for piece in (0, 1):
            z_copy(2 * u + 1, 0, 1, piece).wait_recv()

            @pl.when(u < UNITS - 1)
            def _():
                z_copy(2 * u + 3, 2 * u + 1, 1, piece).start()

        turn = lax.broadcasted_iota(jnp.int32, (CAP, TOK), 0)
        ids = (((x + turn) & (NX - 1)) * NZ + z).astype(F32)
        for i in (0, 1):
            r = 2 * u + i
            meta = zbuf[r, pl.ds(TOK, META)].astype(F32)
            slot, gate = slots_of(meta, ids, tri[...])
            hot, weighted = place_rows(slot, gate * (1.0 / 64.0), 0)
            for first, pick, base in ((0, hot, 0), (PART, weighted, TOK + META)):
                picked = jnp.dot(
                    pick.astype(BF16), zbuf[r, pl.ds(base, TOK)], preferred_element_type=F32
                ).astype(BF16)
                rows[ex, r, 0, :, pl.ds(first, PART)] = picked[:CAP]
                for dx in range(1, NX):
                    xs[dx - 1, r, :, pl.ds(first, PART)] = picked[dx * CAP : (dx + 1) * CAP]
        for dx in range(1, NX):
            x_copy(u, dx).start()

    def spread(u):
        for dx in range(1, NX):
            x_copy(u, dx).wait_recv()
        y1_copy(u, 0).start()
        y1_copy(u, 1).start()
        core_copy(u, 0).start()

    def pass_on(u):
        for k in (0, 1):
            y1_copy(u, k).wait_recv()
            y2_copy(u, k).start()
            core_copy(u, 1 + k).start()

    def far_side(u):
        for k in (0, 1):
            y2_copy(u, k).wait_recv()
        core_copy(u, 3).start()

    def from_core(u):
        for k in range(4):
            core_copy(u, k).wait_recv()

    p_copy = lambda g: remote(
        pall.at[g, :, 1 - core], pr.at[g], rps.at[g], rpr.at[g], (dp, partner)
    )
    half = HPAD // 2

    def compute(g):
        pre = jnp.zeros((HPAD, HPAD), F32)
        back = jnp.zeros((HPAD, HPAD), F32)
        nt = (((1,), (1,)), ((), ()))
        for i in range(8):
            block = rows[i, pl.ds(4 * g, 4)].reshape(HPAD, 2 * PART)
            cols = pl.ds(i * PART, PART)
            pre = pre + lax.dot_general(block[:, :PART], up[:, cols], nt, preferred_element_type=F32)
            back = back + lax.dot_general(block[:, PART:], down[:, cols], nt, preferred_element_type=F32)
        sig = 1.0 / (1.0 + jnp.exp(-pre))
        hidden = pre * sig
        gpre = back * sig * (1.0 + pre * (1.0 - sig))
        at = pl.ds(pl.multiple_of(g * HPAD, HPAD), HPAD)
        gpre_bf = gpre.astype(BF16)
        for i in range(8):
            cols = pl.ds(i * PART, PART)
            pall[g, i // 2, i % 2] = jnp.dot(gpre_bf, up[:, cols], preferred_element_type=F32).astype(BF16)
        p_copy(g).start()
        hid_t[:, at] = hidden.T.astype(BF16)
        gpre_t[:, at] = gpre.T.astype(BF16)

    lower, upper = pl.ds(0, half), pl.ds(half, half)
    far_copy = lambda g, k: remote(
        q.at[g, yof(2), (lower, upper)[k]], fb.at[k, g], rys.at[g, k], ryr.at[g, k], (dp, exof(1 - 2 * k))
    )
    near_copy = lambda g, k: remote(
        q.at[g, yof(1 - 2 * k), (upper, lower)[k]], db.at[k, g], rys.at[g, 2 + k], ryr.at[g, 2 + k], (dp, exof(1 - 2 * k))
    )
    sum_copy = lambda g, k: remote(
        cs.at[k, g], cr.at[k, g], rys.at[g, 4 + k], ryr.at[g, 4 + k], (dp, exof(1 - 2 * k))
    )

    def core_sum(g):
        p_copy(g).wait_recv()
        for dy in (2, 1, 3, 0):
            at = yof(dy)
            q[g, at] = (pall[g, at, core].astype(F32) + pr[g, at].astype(F32)).astype(BF16)
            if dy == 2:
                far_copy(g, 0).start()
                far_copy(g, 1).start()
            elif dy == 1:
                near_copy(g, 0).start()
            elif dy == 3:
                near_copy(g, 1).start()

    def pair_sum(g):
        for k in (0, 1):
            far_copy(g, k).wait_recv()
            own = q[g, yof(1 - 2 * k), (lower, upper)[k]].astype(F32)
            cs[k, g] = (fb[k, g].astype(F32) + own).astype(BF16)
            sum_copy(g, k).start()

    rx_copy = lambda g, dx: remote(
        ts.at[g, dx - 1], u_buf.at[pl.ds(4 * g, 4), dx], rxs.at[g, dx - 1], rxr.at[g, dx - 1], (xz(-dx, 0), ex)
    )

    def full_sum(g):
        for k in (0, 1):
            near_copy(g, k).wait_recv()
            sum_copy(g, k).wait_recv()
        for k in (0, 1):
            own = q[g, y, (lower, upper)[k]].astype(F32)
            total = own + db[1 - k, g].astype(F32) + cr[k, g].astype(F32)
            total = total.astype(BF16).reshape(2, NX, CAP, PART)
            for i in (0, 1):
                u_buf[4 * g + 2 * k + i, 0] = total[i, 0]
                for dx in range(1, NX):
                    ts[g, dx - 1, 2 * k + i] = total[i, dx]
        for dx in range(1, NX):
            rx_copy(g, dx).start()

    def rz_copy(r, step):
        return remote(u_buf.at[r], v_buf.at[r], rzs.at[r], rzr.at[r], (xz(0, step), ex))

    def give_back(g):
        for dx in range(1, NX):
            rx_copy(g, dx).wait_recv()
        for i in (0, 1):
            u = 2 * g + i

            @pl.when(u == 0)
            def _():
                v_buf[0] = u_buf[0]

            @pl.when(u > 0)
            def _():
                rz_copy(2 * u, u).start()

            rz_copy(2 * u + 1, -(u + 1)).start()

    tn = (((1,), (0,)), ((), ()))

    def weight_grads(part):
        for i in (0, 1):
            e = 2 * part + i
            cols = pl.ds(pl.multiple_of(e * PART, PART), PART)
            for first, left, out in ((0, gpre_t, gup), (PART, hid_t, gdown)):
                right = rows[e, :, :, :, pl.ds(first, PART)].reshape(ROWS, PART)
                out[:, cols] = lax.dot_general(
                    left[pl.ds(0, HID)], right, tn, preferred_element_type=F32
                ).astype(BF16)

    @pl.loop(0, 2 * UNITS)
    def _(s):
        @pl.when(s < UNITS)
        def _():
            arrive(s)

        @pl.when(jnp.logical_and(s >= 1, s < UNITS + 1))
        def _():
            spread(s - 1)

        @pl.when(jnp.logical_and(s >= 2, s < UNITS + 2))
        def _():
            pass_on(s - 2)

        @pl.when(jnp.logical_and(s >= 3, s < UNITS + 3))
        def _():
            far_side(s - 3)

        @pl.when(s == 3)
        def _():
            load_up.wait()
            load_down.wait()

        @pl.when(jnp.logical_and(s >= 4, s < UNITS + 4))
        def _():
            from_core(s - 4)

        odd = lax.rem(s, 2) == 1

        @pl.when(jnp.logical_and(odd, jnp.logical_and(s >= 5, s < 13)))
        def _():
            compute((s - 5) // 2)

        @pl.when(s >= 12)
        def _():
            weight_grads(s - 12)

        @pl.when(jnp.logical_and(jnp.logical_not(odd), jnp.logical_and(s >= 6, s < 14)))
        def _():
            core_sum((s - 6) // 2)

        @pl.when(jnp.logical_and(odd, jnp.logical_and(s >= 7, s < 15)))
        def _():
            pair_sum((s - 7) // 2)

        @pl.when(jnp.logical_and(jnp.logical_not(odd), s >= 8))
        def _():
            full_sum((s - 8) // 2)

        @pl.when(jnp.logical_and(odd, s >= 9))
        def _():
            give_back((s - 9) // 2)

        @pl.when(s == 4)
        def _():
            meta = zbuf[0, pl.ds(TOK, META)].astype(F32)
            line = lax.broadcasted_iota(jnp.int32, (4 * NZ, TOK), 0)
            r, dx = line // NX, line & (NX - 1)
            away = jnp.where((r & 1) == 0, r // 2, NZ - (r + 1) // 2)
            ids = ((x + dx) & (NX - 1)) * NZ + ((z + NZ - away) & (NZ - 1))
            slot, _ = slots_of(meta, ids.astype(F32), tri[...])
            for u in range(UNITS):
                hot = [place_rows(slot, None, NX * (2 * u + i))[0] for i in (0, 1)]
                own_hot[u] = jnp.concatenate(hot, axis=0).T.astype(BF16)

    put_up = pltpu.make_async_copy(gup, gup_out, out_sem.at[0])
    put_down = pltpu.make_async_copy(gdown, gdown_out, out_sem.at[1])
    put_up.start()
    put_down.start()
    total = jnp.zeros((TOK, PART), F32)
    for u in range(UNITS):
        if u:
            rz_copy(2 * u, u).wait_recv()
        rz_copy(2 * u + 1, -(u + 1)).wait_recv()
        total = total + jnp.dot(
            own_hot[u], v_buf[pl.ds(2 * u, 2)].reshape(TOK, PART), preferred_element_type=F32
        )
    gtok[...] = total
    put_tok = pltpu.make_async_copy(gtok, gtok_out, out_sem.at[2])
    put_tok.start()

    @pl.loop(0, UNITS)
    def _(u):
        for dx in range(1, NX):
            x_copy(u, dx).wait_send()
        for k in (0, 1):
            y1_copy(u, k).wait_send()
            y2_copy(u, k).wait_send()
        for k in range(4):
            core_copy(u, k).wait_send()
        rz_copy(2 * u + 1, 0).wait_send()
        for piece in (0, 1):
            z_copy(2 * u + 1, 0, 1, piece).wait_send()

        @pl.when(u > 0)
        def _():
            rz_copy(2 * u, 0).wait_send()
            for piece in (0, 1):
                z_copy(2 * u, 0, -1, piece).wait_send()

    @pl.loop(0, GROUPS)
    def _(g):
        p_copy(g).wait_send()
        for k in (0, 1):
            far_copy(g, k).wait_send()
            near_copy(g, k).wait_send()
            sum_copy(g, k).wait_send()
        for dx in range(1, NX):
            rx_copy(g, dx).wait_send()

    for put in (put_up, put_down, put_tok):
        put.wait()


def local(tokens, arms, arm_bias, routes, gates, up_weight, down_weight, cotangent):
    pad = ((0, META - TOPK), (0, 0))
    meta = jnp.concatenate(
        [jnp.pad(routes.T, pad, constant_values=-1), jnp.pad(gates.T, pad)], axis=1
    ).astype(BF16)
    any_space = pl.BlockSpec(memory_space=pl.ANY)
    vmem = pl.BlockSpec(memory_space=pltpu.VMEM)
    dma = pltpu.SemaphoreType.DMA
    pair = lambda *shape: [dma(shape), dma(shape)]
    grad_tokens, grad_up, grad_down = pl.pallas_call(
        kernel,
        out_shape=(
            jax.ShapeDtypeStruct((TOK, PART), F32),
            jax.ShapeDtypeStruct((HID, WIDTH), BF16),
            jax.ShapeDtypeStruct((HID, WIDTH), BF16),
        ),
        in_specs=[any_space, vmem, vmem, any_space, any_space, any_space, any_space],
        out_specs=(any_space, any_space, any_space),
        scratch_shapes=[
            pltpu.VMEM((TOK, PART), BF16),
            pltpu.VMEM((NZ, 2 * TOK + META, PART), BF16),
            pltpu.VMEM((NX - 1, NZ, CAP, 2 * PART), BF16),
            pltpu.VMEM((8, NZ, NX, CAP, 2 * PART), BF16),
            pltpu.VMEM((HPAD, WIDTH), BF16),
            pltpu.VMEM((HPAD, WIDTH), BF16),
            pltpu.VMEM((HPAD, ROWS), BF16),
            pltpu.VMEM((HPAD, ROWS), BF16),
            pltpu.VMEM((GROUPS, NY, 2, HPAD, PART), BF16),
            pltpu.VMEM((GROUPS, NY, HPAD, PART), BF16),
            pltpu.VMEM((GROUPS, NY, HPAD, PART), BF16),
            pltpu.VMEM((2, GROUPS, HPAD // 2, PART), BF16),
            pltpu.VMEM((2, GROUPS, HPAD // 2, PART), BF16),
            pltpu.VMEM((2, GROUPS, HPAD // 2, PART), BF16),
            pltpu.VMEM((2, GROUPS, HPAD // 2, PART), BF16),
            pltpu.VMEM((GROUPS, NX - 1, 4, CAP, PART), BF16),
            pltpu.VMEM((NZ, NX, CAP, PART), BF16),
            pltpu.VMEM((NZ, NX, CAP, PART), BF16),
            pltpu.VMEM((HID, WIDTH), BF16),
            pltpu.VMEM((HID, WIDTH), BF16),
            pltpu.VMEM((TOK, PART), F32),
            pltpu.VMEM((TOK, TOK), BF16),
            pltpu.VMEM((UNITS, TOK, TOK), BF16),
            dma((5,)),
            dma((3,)),
            *pair(NZ, 2),
            *pair(UNITS, NX - 1),
            *pair(UNITS, 2),
            *pair(UNITS, 2),
            *pair(UNITS, 4),
            *pair(GROUPS),
            *pair(GROUPS, 6),
            *pair(GROUPS, NX - 1),
            *pair(NZ),
        ],
        compiler_params=pltpu.CompilerParams(
            collective_id=0, has_side_effects=True, vmem_limit_bytes=56 * 1024 * 1024
        ),
        name="expert_backward",
    )(tokens, arms.reshape(1, TOK), arm_bias, meta, up_weight[0], down_weight[0], cotangent)
    return grad_tokens, grad_up[None], grad_down[None]


def solution(mesh):
    in_specs = (
        P("dp", None),
        P("dp"),
        P(),
        P("dp", None),
        P("dp", None),
        P("dp", "expert", None),
        P("dp", "expert", None),
        P("dp", None),
    )
    out_specs = (P("dp", "expert"), P("dp", "expert", None), P("dp", "expert", None))
    return jax.shard_map(local, mesh=mesh, in_specs=in_specs, out_specs=out_specs, check_vma=False)
```

```python
import jax
import jax.numpy as jnp
from jax import lax
from jax.experimental import pallas as pl
from jax.experimental.pallas import tpu as pltpu
from jax.sharding import PartitionSpec as P

MESH = pl.DeviceIdType.MESH
F32, BF16 = jnp.float32, jnp.bfloat16

TOK = 128
CAP = 16
PART = 256
HID = 176
HPAD = 256
PAIR = 128
NX, NY, NZ = 4, 4, 16
META = 16
TOPK = 6
UNITS = 8
SLOT = 64
ROWS = 1024
WIDTH = 2048

ORDER = (
    ("A", 0), ("Z", 1), ("B", 0), ("Z", 2), ("A", 1), ("A", 2), ("Z", 3), ("C", 0), ("A", 3), ("B", 1),
    ("Z", 4), ("A", 4), ("B", 2), ("Z", 5), ("A", 5), ("B", 3), ("Z", 6), ("B", 4), ("Z", 7), ("C", 1),
    ("B", 5), ("C", 3), ("A", 7), ("Z", 8), ("C", 4), ("C", 2), ("A", 8), ("Z", 9), ("A", 9), ("B", 7),
    ("Z", 10), ("B", 8), ("A", 10), ("D", 4), ("D", 2), ("B", 9), ("C", 5), ("Z", 11), ("D", 0), ("A", 11),
    ("Z", 12), ("C", 8), ("A", 12), ("D", 1), ("B", 10), ("C", 9), ("D", 5), ("Z", 13), ("B", 11), ("D", 8),
    ("A", 13), ("C", 10), ("A", 6), ("D", 9), ("C", 7), ("B", 12), ("Z", 14), ("A", 14), ("C", 11), ("F", 4),
    ("B", 13), ("D", 10), ("Z", 15), ("C", 12), ("A", 15), ("B", 14), ("G", 4), ("D", 11), ("C", 13), ("F", 2),
    ("B", 15), ("F", 5), ("H", 4), ("D", 12), ("D", 13), ("D", 3), ("G", 2), ("F", 0), ("G", 5), ("I", 4),
    ("H", 2), ("C", 15), ("F", 6), ("C", 14), ("H", 5), ("B", 6), ("I", 2), ("J", 4), ("G", 6), ("D", 15),
    ("D", 14), ("D", 7), ("F", 1), ("I", 5), ("F", 7), ("C", 6), ("J", 2), ("H", 6), ("J", 5), ("D", 6),
    ("G", 7), ("I", 6), ("F", 3), ("H", 7), ("G", 1), ("J", 6), ("G", 3), ("I", 7), ("G", 0), ("H", 3),
    ("J", 7), ("H", 1), ("H", 0), ("I", 3), ("O", 0), ("W", 4), ("I", 1), ("W", 0), ("I", 0), ("J", 3),
    ("J", 1), ("W", 7), ("W", 6), ("W", 5), ("W", 1), ("J", 0), ("W", 2), ("W", 3),
)


def place_rows(slot, gate, first):
    index = lax.broadcasted_iota(jnp.int32, (CAP, TOK), 0).astype(F32)
    hot, weighted = [], []
    for i in range(NX):
        here = jnp.broadcast_to(slot[first + i : first + i + 1], (CAP, TOK)) == index
        hot.append(jnp.where(here, 1.0, 0.0))
        if gate is not None:
            weight = jnp.broadcast_to(gate[first + i : first + i + 1], (CAP, TOK))
            weighted.append(jnp.where(here, weight, 0.0))
    hot = jnp.concatenate(hot, axis=0)
    return hot, (jnp.concatenate(weighted, axis=0) if weighted else None)


def slots_of(meta, ids, earlier):
    hits = jnp.zeros(ids.shape, F32)
    gate = jnp.zeros(ids.shape, F32)
    for k in range(TOPK):
        same = jnp.broadcast_to(meta[k : k + 1, :TOK], ids.shape) == ids
        hits = hits + jnp.where(same, 1.0, 0.0)
        gate = gate + jnp.where(same, jnp.broadcast_to(meta[k : k + 1, TOK:], ids.shape), 0.0)
    rank = jnp.dot(hits.astype(BF16), earlier, preferred_element_type=F32)
    return jnp.where(hits > 0.5, rank, -1.0), gate


def kernel(
    tokens, arms_in, bias_in, routes_in, gates_in, up_in, down_in, cot,
    gtok, gup, gdown,
    tok, arms, bias, routes, gates, zbuf, xs, rows, up, down, hid_t, gpre_t, pall, pr, q, fb, db, cs, cr, ts,
    u_buf, v_buf, tri, own_hot,
    in_sem, zs, zr, xsem, xrem, y1s, y1r, y2s, y2r, cos, cor, rps, rpr, rys, ryr, rxs, rxr, rzs, rzr,
):
    dp, ex = lax.axis_index("dp"), lax.axis_index("expert")
    x, z = dp // NZ, lax.rem(dp, NZ)
    y, core = ex // 2, lax.rem(ex, 2)
    xz = lambda dx, dz: lax.rem(x + dx + NX, NX) * NZ + lax.rem(z + dz + NZ, NZ)
    yof = lambda dy: lax.rem(y + dy + NY, NY)
    exof = lambda dy: yof(dy) * 2 + core
    partner = y * 2 + (1 - core)

    def remote(src, dst, send, recv, to):
        return pltpu.make_async_remote_copy(
            src_ref=src, dst_ref=dst, send_sem=send, recv_sem=recv, device_id=to, device_id_type=MESH
        )

    lanes = pl.ds(pl.multiple_of(ex * PART, PART), PART)
    local_copy = lambda src, dst, i: pltpu.make_async_copy(src, dst, in_sem.at[i])
    load_tok = local_copy(tokens.at[:, lanes], tok, 0)
    load_cot = local_copy(cot.at[:, lanes], zbuf.at[0, pl.ds(TOK + META, TOK)], 1)
    load_up = local_copy(up_in, up.at[pl.ds(0, HID)], 2)
    load_down = local_copy(down_in, down.at[pl.ds(0, HID)], 3)
    load_small = [
        local_copy(arms_in, arms, 4), local_copy(bias_in, bias, 5),
        local_copy(routes_in, routes, 6), local_copy(gates_in, gates, 7),
    ]
    for load in (*load_small, load_tok, load_cot):
        load.start()

    barrier = pltpu.get_barrier_semaphore()
    peers = [(xz(d, 0), ex) for d in (1, 2, 3)]
    peers += [(xz(0, 1), ex), (xz(0, -1), ex), (dp, exof(1)), (dp, exof(-1)), (dp, partner)]
    for to in peers:
        pl.semaphore_signal(barrier, inc=1, device_id=to, device_id_type=MESH)

    tri[...] = jnp.where(
        lax.broadcasted_iota(jnp.int32, (TOK, TOK), 0) < lax.broadcasted_iota(jnp.int32, (TOK, TOK), 1), 1.0, 0.0
    ).astype(BF16)
    for load in load_small:
        load.wait()
    arm_row = jnp.broadcast_to(arms[...], (TOK, TOK))
    arm_hot = jnp.where(arm_row == lax.broadcasted_iota(jnp.int32, (TOK, TOK), 0), 1.0, 0.0).T
    own_bias = bias[:, lanes].astype(F32)
    added = jnp.zeros((TOK, PART), F32)
    for a in range(own_bias.shape[0]):
        added = added + arm_hot[:, a : a + 1] * own_bias[a : a + 1]
    line = lax.broadcasted_iota(jnp.int32, (META, TOK), 0)
    for at, table in ((0, routes), (TOK, gates)):
        packed = jnp.zeros((META, TOK), F32)
        for k in range(TOPK):
            packed = jnp.where(line == k, jnp.broadcast_to(table[k : k + 1].astype(F32), (META, TOK)), packed)
        zbuf[0, pl.ds(TOK, META), pl.ds(at, TOK)] = packed.astype(BF16)
    load_tok.wait()
    zbuf[0, pl.ds(0, TOK)] = (tok[...].astype(F32) + added).astype(BF16)
    load_cot.wait()
    pl.semaphore_wait(barrier, len(peers))

    pieces = ((0, TOK + META), (TOK + META, TOK))

    def z_copy(to_slot, piece):
        at = pl.ds(*pieces[piece])
        step = 1 if to_slot % 2 else -1
        return remote(
            zbuf.at[max(to_slot - 2, 0), at], zbuf.at[to_slot, at],
            zs.at[to_slot, piece], zr.at[to_slot, piece], (xz(0, step), ex),
        )

    for piece in (0, 1):
        z_copy(1, piece).start()
        z_copy(2, piece).start()
    load_up.start()
    load_down.start()
    up[pl.ds(HID, HPAD - HID)] = jnp.zeros((HPAD - HID, WIDTH), BF16)
    down[pl.ds(HID, HPAD - HID)] = jnp.zeros((HPAD - HID, WIDTH), BF16)

    x_copy = lambda r, dx: remote(
        xs.at[dx - 1, r], rows.at[ex, r, dx], xsem.at[r, dx - 1], xrem.at[r, dx - 1], (xz(dx, 0), ex)
    )
    y1_copy = lambda r, k: remote(
        rows.at[ex, r], rows.at[ex, r], y1s.at[r, k], y1r.at[r, k], (dp, exof(1 - 2 * k))
    )

    def y2_copy(r, k):
        part = rows.at[exof(2 * k - 1), r, pl.ds(2 * k, 2)]
        return remote(part, part, y2s.at[r, k], y2r.at[r, k], (dp, exof(1 - 2 * k)))

    def core_copy(r, k):
        part = rows.at[exof((0, -1, 1, 2)[k]), r]
        return remote(part, part, cos.at[r, k], cor.at[r, k], (dp, partner))

    turn = lax.broadcasted_iota(jnp.int32, (CAP, TOK), 0)
    here = (((x + turn) & (NX - 1)) * NZ + z).astype(F32)

    def arrive(r):
        for piece in (0, 1):
            z_copy(r, piece).wait_recv()
            if r + 2 < NZ:
                z_copy(r + 2, piece).start()

    def pick(r):
        meta = zbuf[r, pl.ds(TOK, META)].astype(F32)
        slot, gate = slots_of(meta, here, tri[...])
        hot, weighted = place_rows(slot, gate * (1.0 / 64.0), 0)
        for first, chosen, base in ((0, hot, 0), (PART, weighted, TOK + META)):
            picked = jnp.dot(
                chosen.astype(BF16), zbuf[r, pl.ds(base, TOK)], preferred_element_type=F32
            ).astype(BF16)
            rows[ex, r, 0, :, pl.ds(first, PART)] = picked[:CAP]
            for dx in range(1, NX):
                xs[dx - 1, r, :, pl.ds(first, PART)] = picked[dx * CAP : (dx + 1) * CAP]
        for dx in range(1, NX):
            x_copy(r, dx).start()

    def spread(r):
        for dx in range(1, NX):
            x_copy(r, dx).wait_recv()
        y1_copy(r, 0).start()
        y1_copy(r, 1).start()
        core_copy(r, 0).start()

    def pass_on(r):
        for k in (0, 1):
            y1_copy(r, k).wait_recv()
            y2_copy(r, k).start()
            core_copy(r, 1 + k).start()

    def far_side(r):
        for k in (0, 1):
            y2_copy(r, k).wait_recv()
        core_copy(r, 3).start()

    p_copy = lambda u: remote(pall.at[u, :, 1 - core], pr.at[u], rps.at[u], rpr.at[u], (dp, partner))

    def compute(u):
        for r in (2 * u, 2 * u + 1):
            for k in range(4):
                core_copy(r, k).wait_recv()
        pre = jnp.zeros((PAIR, HPAD), F32)
        back = jnp.zeros((PAIR, HPAD), F32)
        nt = (((1,), (1,)), ((), ()))
        for i in range(8):
            block = rows[i, pl.ds(2 * u, 2)].reshape(PAIR, 2 * PART)
            cols = pl.ds(i * PART, PART)
            pre = pre + lax.dot_general(block[:, :PART], up[:, cols], nt, preferred_element_type=F32)
            back = back + lax.dot_general(block[:, PART:], down[:, cols], nt, preferred_element_type=F32)
        sig = 1.0 / (1.0 + jnp.exp(-pre))
        hidden = pre * sig
        gpre = back * sig * (1.0 + pre * (1.0 - sig))
        gpre_bf = gpre.astype(BF16)
        for i in range(8):
            cols = pl.ds(i * PART, PART)
            pall[u, i // 2, i % 2] = jnp.dot(gpre_bf, up[:, cols], preferred_element_type=F32).astype(BF16)
        p_copy(u).start()
        hid_t[:, pl.ds(u * PAIR, PAIR)] = hidden.T.astype(BF16)
        gpre_t[:, pl.ds(u * PAIR, PAIR)] = gpre.T.astype(BF16)

    halves = (pl.ds(0, SLOT), pl.ds(SLOT, SLOT))
    far_copy = lambda u, k: remote(
        q.at[u, yof(2), halves[k]], fb.at[k, u], rys.at[u, k], ryr.at[u, k], (dp, exof(1 - 2 * k))
    )
    near_copy = lambda u, k: remote(
        q.at[u, yof(1 - 2 * k), halves[1 - k]], db.at[k, u], rys.at[u, 2 + k], ryr.at[u, 2 + k], (dp, exof(1 - 2 * k))
    )
    sum_copy = lambda u, k: remote(
        cs.at[k, u], cr.at[k, u], rys.at[u, 4 + k], ryr.at[u, 4 + k], (dp, exof(1 - 2 * k))
    )

    def core_sum(u):
        p_copy(u).wait_recv()
        for dy in (2, 1, -1, 0):
            at = yof(dy)
            q[u, at] = (pall[u, at, core].astype(F32) + pr[u, at].astype(F32)).astype(BF16)
            if dy == 2:
                far_copy(u, 0).start()
                far_copy(u, 1).start()
            elif dy == 1:
                near_copy(u, 0).start()
            elif dy == -1:
                near_copy(u, 1).start()

    def pair_sum(u):
        for k in (0, 1):
            far_copy(u, k).wait_recv()
            own = q[u, yof(1 - 2 * k), halves[k]].astype(F32)
            cs[k, u] = (fb[k, u].astype(F32) + own).astype(BF16)
            sum_copy(u, k).start()

    rx_copy = lambda u, dx: remote(
        ts.at[u, dx - 1], u_buf.at[pl.ds(2 * u, 2), dx], rxs.at[u, dx - 1], rxr.at[u, dx - 1], (xz(-dx, 0), ex)
    )

    def full_sum(u):
        for k in (0, 1):
            near_copy(u, k).wait_recv()
            sum_copy(u, k).wait_recv()
        for k in (0, 1):
            own = q[u, y, halves[k]].astype(F32)
            total = own + db[1 - k, u].astype(F32) + cr[k, u].astype(F32)
            total = total.astype(BF16).reshape(NX, CAP, PART)
            u_buf[2 * u + k, 0] = total[0]
            for dx in range(1, NX):
                ts[u, dx - 1, k] = total[dx]
        for dx in range(1, NX):
            rx_copy(u, dx).start()

    def rz_copy(r):
        step = -(r + 1) // 2 if r % 2 else r // 2
        return remote(u_buf.at[r], v_buf.at[r], rzs.at[r], rzr.at[r], (xz(0, step), ex))

    def give_back(u):
        for dx in range(1, NX):
            rx_copy(u, dx).wait_recv()
        if u == 0:
            v_buf[0] = u_buf[0]
        else:
            rz_copy(2 * u).start()
        rz_copy(2 * u + 1).start()

    tn = (((1,), (0,)), ((), ()))

    def weight_grads(e):
        cols = pl.ds(e * PART, PART)
        for first, left, out in ((0, gpre_t, gup), (PART, hid_t, gdown)):
            right = rows[e, :, :, :, pl.ds(first, PART)].reshape(ROWS, PART)
            out[:, cols] = lax.dot_general(
                left[pl.ds(0, HID)], right, tn, preferred_element_type=F32
            ).astype(BF16)

    def own_places(_):
        meta = zbuf[0, pl.ds(TOK, META)].astype(F32)
        line = lax.broadcasted_iota(jnp.int32, (4 * NZ, TOK), 0)
        r, dx = line // NX, line & (NX - 1)
        away = jnp.where((r & 1) == 0, r // 2, NZ - (r + 1) // 2)
        ids = ((x + dx) & (NX - 1)) * NZ + ((z + NZ - away) & (NZ - 1))
        slot, _ = slots_of(meta, ids.astype(F32), tri[...])
        for u in range(UNITS):
            hot = [place_rows(slot, None, NX * (2 * u + i))[0] for i in (0, 1)]
            own_hot[u] = jnp.concatenate(hot, axis=0).T.astype(BF16)

    steps = dict(
        Z=arrive, A=pick, B=spread, C=pass_on, D=far_side, F=compute, G=core_sum, H=pair_sum, I=full_sum,
        J=give_back, W=weight_grads, O=own_places,
    )
    first_matmul = next(i for i, (name, _) in enumerate(ORDER) if name == "F")
    for i, (name, which) in enumerate(ORDER):
        if i == first_matmul:
            load_up.wait()
            load_down.wait()
        steps[name](which)

    total = jnp.zeros((TOK, PART), F32)
    for u in [which for name, which in ORDER if name == "J"]:
        if u:
            rz_copy(2 * u).wait_recv()
        rz_copy(2 * u + 1).wait_recv()
        total = total + jnp.dot(
            own_hot[u], v_buf[pl.ds(2 * u, 2)].reshape(TOK, PART), preferred_element_type=F32
        )
    gtok[...] = total

    for r in range(NZ):
        for dx in range(1, NX):
            x_copy(r, dx).wait_send()
        for k in (0, 1):
            y1_copy(r, k).wait_send()
            y2_copy(r, k).wait_send()
        for k in range(4):
            core_copy(r, k).wait_send()
        if r:
            rz_copy(r).wait_send()
            for piece in (0, 1):
                z_copy(r, piece).wait_send()
    for u in range(UNITS):
        p_copy(u).wait_send()
        for k in (0, 1):
            far_copy(u, k).wait_send()
            near_copy(u, k).wait_send()
            sum_copy(u, k).wait_send()
        for dx in range(1, NX):
            rx_copy(u, dx).wait_send()


def put_out(gtok, gup, gdown, gtok_out, gup_out, gdown_out, sem):
    copies = [
        pltpu.make_async_copy(src, dst, sem.at[i])
        for i, (src, dst) in enumerate(((gup, gup_out), (gdown, gdown_out), (gtok, gtok_out)))
    ]
    for copy in copies:
        copy.start()
    for copy in copies:
        copy.wait()


def local(tokens, arms, arm_bias, routes, gates, up_weight, down_weight, cotangent):
    hbm = pl.BlockSpec(memory_space=pltpu.HBM)
    vmem = pl.BlockSpec(memory_space=pltpu.VMEM)
    dma = pltpu.SemaphoreType.DMA
    pair = lambda *shape: [dma(shape), dma(shape)]
    out_shape = (
        jax.ShapeDtypeStruct((TOK, PART), F32),
        jax.ShapeDtypeStruct((HID, WIDTH), BF16),
        jax.ShapeDtypeStruct((HID, WIDTH), BF16),
    )
    operands = (
        tokens, arms.reshape(1, TOK), arm_bias, routes.T, gates.T, up_weight[0], down_weight[0], cotangent
    )
    results = pl.pallas_call(
        kernel,
        out_shape=out_shape,
        in_specs=[hbm] * 8,
        out_specs=(vmem, vmem, vmem),
        scratch_shapes=[
            pltpu.VMEM((TOK, PART), BF16),
            pltpu.VMEM((1, TOK), jnp.int32),
            pltpu.VMEM(arm_bias.shape, BF16),
            pltpu.VMEM((TOPK, TOK), jnp.int32),
            pltpu.VMEM((TOPK, TOK), jnp.int32),
            pltpu.VMEM((NZ, 2 * TOK + META, PART), BF16),
            pltpu.VMEM((NX - 1, NZ, CAP, 2 * PART), BF16),
            pltpu.VMEM((8, NZ, NX, CAP, 2 * PART), BF16),
            pltpu.VMEM((HPAD, WIDTH), BF16),
            pltpu.VMEM((HPAD, WIDTH), BF16),
            pltpu.VMEM((HPAD, ROWS), BF16),
            pltpu.VMEM((HPAD, ROWS), BF16),
            pltpu.VMEM((UNITS, NY, 2, PAIR, PART), BF16),
            pltpu.VMEM((UNITS, NY, PAIR, PART), BF16),
            pltpu.VMEM((UNITS, NY, PAIR, PART), BF16),
            pltpu.VMEM((2, UNITS, SLOT, PART), BF16),
            pltpu.VMEM((2, UNITS, SLOT, PART), BF16),
            pltpu.VMEM((2, UNITS, SLOT, PART), BF16),
            pltpu.VMEM((2, UNITS, SLOT, PART), BF16),
            pltpu.VMEM((UNITS, NX - 1, 2, CAP, PART), BF16),
            pltpu.VMEM((NZ, NX, CAP, PART), BF16),
            pltpu.VMEM((NZ, NX, CAP, PART), BF16),
            pltpu.VMEM((TOK, TOK), BF16),
            pltpu.VMEM((UNITS, TOK, TOK), BF16),
            dma((8,)),
            *pair(NZ, 2),
            *pair(NZ, NX - 1),
            *pair(NZ, 2),
            *pair(NZ, 2),
            *pair(NZ, 4),
            *pair(UNITS),
            *pair(UNITS, 6),
            *pair(UNITS, NX - 1),
            *pair(NZ),
        ],
        compiler_params=pltpu.CompilerParams(
            collective_id=0, has_side_effects=True, vmem_limit_bytes=36 * 1024 * 1024
        ),
        name="expert_backward",
    )(*(pltpu.with_memory_space_constraint(a, pltpu.HBM) for a in operands))
    grad_tokens, grad_up, grad_down = pl.pallas_call(
        put_out,
        out_shape=out_shape,
        in_specs=[vmem] * 3,
        out_specs=(hbm, hbm, hbm),
        scratch_shapes=[dma((3,))],
        compiler_params=pltpu.CompilerParams(vmem_limit_bytes=4 * 1024 * 1024),
        name="put_out",
    )(*results)
    return grad_tokens, grad_up[None], grad_down[None]


def solution(mesh):
    in_specs = (
        P("dp", None),
        P("dp"),
        P(),
        P("dp", None),
        P("dp", None),
        P("dp", "expert", None),
        P("dp", "expert", None),
        P("dp", None),
    )
    out_specs = (P("dp", "expert"), P("dp", "expert", None), P("dp", "expert", None))
    return jax.shard_map(local, mesh=mesh, in_specs=in_specs, out_specs=out_specs, check_vma=False)
```

```python
import jax
import jax.numpy as jnp
from jax import lax
from jax.experimental import pallas as pl
from jax.experimental.pallas import tpu as pltpu
from jax.sharding import PartitionSpec as P

MESH = pl.DeviceIdType.MESH
F32, BF16 = jnp.float32, jnp.bfloat16

TOK = 128
CAP = 16
PART = 256
HID = 176
HPAD = 256
PAIR = 128
NX, NY, NZ = 4, 4, 16
META = 16
TOPK = 6
UNITS = 8
SLOT = 64
ROWS = 1024
WIDTH = 2048

ORDER = (
    ("A", 0), ("Z", 4), ("Z", 2), ("B", 0), ("Z", 5), ("Z", 3), ("A", 2), ("C", 0), ("A", 1), ("Z", 6),
    ("Z", 8), ("Z", 9), ("Z", 7), ("A", 4), ("B", 2), ("A", 3), ("B", 1), ("Z", 12), ("Z", 10), ("Z", 13),
    ("Z", 11), ("C", 2), ("B", 4), ("A", 5), ("D", 0), ("A", 6), ("C", 1), ("B", 3), ("Z", 16), ("Z", 14),
    ("Z", 17), ("Z", 15), ("C", 4), ("A", 7), ("A", 8), ("B", 5), ("Z", 20), ("B", 6), ("Z", 18), ("D", 4),
    ("Z", 19), ("C", 3), ("D", 2), ("Z", 21), ("A", 10), ("B", 7), ("B", 8), ("Z", 22), ("C", 6), ("A", 9),
    ("D", 3), ("Z", 23), ("C", 7), ("A", 11), ("C", 5), ("Z", 24), ("Z", 25), ("B", 10), ("A", 12), ("D", 7),
    ("B", 9), ("D", 6), ("Z", 27), ("Z", 26), ("B", 11), ("D", 5), ("Z", 29), ("Z", 28), ("C", 10), ("A", 13),
    ("D", 1), ("B", 12), ("F", 3), ("A", 14), ("C", 11), ("G", 3), ("F", 1), ("Z", 30), ("B", 13), ("D", 10),
    ("Z", 31), ("A", 15), ("D", 11), ("C", 12), ("B", 14), ("F", 5), ("C", 13), ("F", 0), ("D", 12), ("B", 15),
    ("H", 3), ("G", 5), ("D", 13), ("F", 2), ("C", 14), ("F", 6), ("C", 15), ("I", 3), ("O", 0), ("H", 5),
    ("G", 6), ("C", 8), ("D", 15), ("D", 14), ("C", 9), ("I", 5), ("J", 3), ("H", 6), ("F", 7), ("G", 1),
    ("D", 9), ("D", 8), ("G", 7), ("J", 5), ("I", 6), ("F", 4), ("H", 7), ("G", 4), ("W", 2), ("J", 6),
    ("I", 7), ("W", 1), ("W", 5), ("H", 4), ("G", 0), ("G", 2), ("H", 1), ("I", 4), ("J", 7), ("W", 6),
    ("H", 0), ("H", 2), ("I", 2), ("J", 4), ("I", 1), ("I", 0), ("J", 2), ("W", 7), ("J", 1), ("J", 0),
    ("W", 0), ("W", 3), ("W", 4),
)


def place_rows(slot, gate, first):
    index = lax.broadcasted_iota(jnp.int32, (CAP, TOK), 0).astype(F32)
    hot, weighted = [], []
    for i in range(NX):
        here = jnp.broadcast_to(slot[first + i : first + i + 1], (CAP, TOK)) == index
        hot.append(jnp.where(here, 1.0, 0.0))
        if gate is not None:
            weight = jnp.broadcast_to(gate[first + i : first + i + 1], (CAP, TOK))
            weighted.append(jnp.where(here, weight, 0.0))
    hot = jnp.concatenate(hot, axis=0)
    return hot, (jnp.concatenate(weighted, axis=0) if weighted else None)


def slots_of(meta, ids, earlier):
    hits = jnp.zeros(ids.shape, F32)
    gate = jnp.zeros(ids.shape, F32)
    for k in range(TOPK):
        same = jnp.broadcast_to(meta[k : k + 1, :TOK], ids.shape) == ids
        hits = hits + jnp.where(same, 1.0, 0.0)
        gate = gate + jnp.where(same, jnp.broadcast_to(meta[k : k + 1, TOK:], ids.shape), 0.0)
    rank = jnp.dot(hits.astype(BF16), earlier, preferred_element_type=F32)
    return jnp.where(hits > 0.5, rank, -1.0), gate


def kernel(
    tokens, arms_in, bias_in, routes_in, gates_in, up_in, down_in, cot,
    gtok, gup, gdown,
    tok, arms, bias, routes, gates, zbuf, xs, rows, up, down, hid_t, gpre_t, pall, pr, q, fb, db, cs, cr, ts,
    u_buf, v_buf, tri, own_hot,
    in_sem, zs, zr, xsem, xrem, y1s, y1r, y2s, y2r, cos, cor, rps, rpr, rys, ryr, rxs, rxr, rzs, rzr,
):
    dp, ex = lax.axis_index("dp"), lax.axis_index("expert")
    x, z = dp // NZ, lax.rem(dp, NZ)
    y, core = ex // 2, lax.rem(ex, 2)
    xz = lambda dx, dz: lax.rem(x + dx + NX, NX) * NZ + lax.rem(z + dz + NZ, NZ)
    yof = lambda dy: lax.rem(y + dy + NY, NY)
    exof = lambda dy: yof(dy) * 2 + core
    partner = y * 2 + (1 - core)

    def remote(src, dst, send, recv, to):
        return pltpu.make_async_remote_copy(
            src_ref=src, dst_ref=dst, send_sem=send, recv_sem=recv, device_id=to, device_id_type=MESH
        )

    lanes = pl.ds(pl.multiple_of(ex * PART, PART), PART)
    local_copy = lambda src, dst, i: pltpu.make_async_copy(src, dst, in_sem.at[i])
    load_tok = local_copy(tokens.at[:, lanes], tok, 0)
    load_cot = local_copy(cot.at[:, lanes], zbuf.at[0, pl.ds(TOK + META, TOK)], 1)
    load_up = local_copy(up_in, up.at[pl.ds(0, HID)], 2)
    load_down = local_copy(down_in, down.at[pl.ds(0, HID)], 3)
    load_small = [
        local_copy(arms_in, arms, 4), local_copy(bias_in, bias, 5),
        local_copy(routes_in, routes, 6), local_copy(gates_in, gates, 7),
    ]
    for load in (*load_small, load_tok, load_cot):
        load.start()

    barrier = pltpu.get_barrier_semaphore()
    peers = [(xz(d, 0), ex) for d in (1, 2, 3)]
    peers += [(xz(0, 1), ex), (xz(0, -1), ex), (dp, exof(1)), (dp, exof(-1)), (dp, partner)]
    for to in peers:
        pl.semaphore_signal(barrier, inc=1, device_id=to, device_id_type=MESH)

    tri[...] = jnp.where(
        lax.broadcasted_iota(jnp.int32, (TOK, TOK), 0) < lax.broadcasted_iota(jnp.int32, (TOK, TOK), 1), 1.0, 0.0
    ).astype(BF16)
    for load in load_small:
        load.wait()
    arm_row = jnp.broadcast_to(arms[...], (TOK, TOK))
    arm_hot = jnp.where(arm_row == lax.broadcasted_iota(jnp.int32, (TOK, TOK), 0), 1.0, 0.0).T
    own_bias = bias[:, lanes].astype(F32)
    added = jnp.zeros((TOK, PART), F32)
    for a in range(own_bias.shape[0]):
        added = added + arm_hot[:, a : a + 1] * own_bias[a : a + 1]
    line = lax.broadcasted_iota(jnp.int32, (META, TOK), 0)
    for at, table in ((0, routes), (TOK, gates)):
        packed = jnp.zeros((META, TOK), F32)
        for k in range(TOPK):
            packed = jnp.where(line == k, jnp.broadcast_to(table[k : k + 1].astype(F32), (META, TOK)), packed)
        zbuf[0, pl.ds(TOK, META), pl.ds(at, TOK)] = packed.astype(BF16)
    load_tok.wait()
    zbuf[0, pl.ds(0, TOK)] = (tok[...].astype(F32) + added).astype(BF16)
    load_cot.wait()
    pl.semaphore_wait(barrier, len(peers))

    pieces = ((0, TOK + META), (TOK + META, TOK))

    def z_copy(to_slot, piece):
        at = pl.ds(*pieces[piece])
        step = 1 if to_slot % 2 else -1
        return remote(
            zbuf.at[max(to_slot - 2, 0), at], zbuf.at[to_slot, at],
            zs, zr.at[to_slot, piece], (xz(0, step), ex),
        )

    for piece in range(len(pieces)):
        z_copy(1, piece).start()
        z_copy(2, piece).start()
    load_up.start()
    load_down.start()
    up[pl.ds(HID, HPAD - HID)] = jnp.zeros((HPAD - HID, WIDTH), BF16)
    down[pl.ds(HID, HPAD - HID)] = jnp.zeros((HPAD - HID, WIDTH), BF16)

    x_copy = lambda r, dx: remote(
        xs.at[dx - 1, r], rows.at[ex, r, dx], xsem, xrem.at[r, dx - 1], (xz(dx, 0), ex)
    )
    y1_copy = lambda r, k: remote(
        rows.at[ex, r], rows.at[ex, r], y1s, y1r.at[r, k], (dp, exof(1 - 2 * k))
    )

    def y2_copy(r, k):
        part = rows.at[exof(2 * k - 1), r, pl.ds(2 * k, 2)]
        return remote(part, part, y2s, y2r.at[r, k], (dp, exof(1 - 2 * k)))

    def core_copy(r, k):
        part = rows.at[exof((0, -1, 1, 2)[k]), r]
        return remote(part, part, cos, cor.at[r, k], (dp, partner))

    turn = lax.broadcasted_iota(jnp.int32, (CAP, TOK), 0)
    here = (((x + turn) & (NX - 1)) * NZ + z).astype(F32)

    def arrive(which):
        r, piece = which // 2, which % 2
        z_copy(r, piece).wait_recv()
        if r + 2 < NZ:
            z_copy(r + 2, piece).start()

    def pick(r):
        meta = zbuf[r, pl.ds(TOK, META)].astype(F32)
        slot, gate = slots_of(meta, here, tri[...])
        hot, weighted = place_rows(slot, gate * (1.0 / 64.0), 0)
        for first, chosen, base in ((0, hot, 0), (PART, weighted, TOK + META)):
            picked = jnp.dot(
                chosen.astype(BF16), zbuf[r, pl.ds(base, TOK)], preferred_element_type=F32
            ).astype(BF16)
            rows[ex, r, 0, :, pl.ds(first, PART)] = picked[:CAP]
            for dx in range(1, NX):
                xs[dx - 1, r, :, pl.ds(first, PART)] = picked[dx * CAP : (dx + 1) * CAP]
        for dx in range(1, NX):
            x_copy(r, dx).start()

    def spread(r):
        for dx in range(1, NX):
            x_copy(r, dx).wait_recv()
        y1_copy(r, 0).start()
        y1_copy(r, 1).start()
        core_copy(r, 0).start()

    def pass_on(r):
        for k in (0, 1):
            y1_copy(r, k).wait_recv()
            y2_copy(r, k).start()
            core_copy(r, 1 + k).start()

    def far_side(r):
        for k in (0, 1):
            y2_copy(r, k).wait_recv()
        core_copy(r, 3).start()

    p_copy = lambda u: remote(pall.at[u, :, 1 - core], pr.at[u], rps, rpr.at[u], (dp, partner))

    def compute(u):
        for r in (2 * u, 2 * u + 1):
            for k in range(4):
                core_copy(r, k).wait_recv()
        pre = jnp.zeros((PAIR, HPAD), F32)
        back = jnp.zeros((PAIR, HPAD), F32)
        nt = (((1,), (1,)), ((), ()))
        for i in range(8):
            block = rows[i, pl.ds(2 * u, 2)].reshape(PAIR, 2 * PART)
            cols = pl.ds(i * PART, PART)
            pre = pre + lax.dot_general(block[:, :PART], up[:, cols], nt, preferred_element_type=F32)
            back = back + lax.dot_general(block[:, PART:], down[:, cols], nt, preferred_element_type=F32)
        sig = 1.0 / (1.0 + jnp.exp(-pre))
        hidden = pre * sig
        gpre = back * sig * (1.0 + pre * (1.0 - sig))
        gpre_bf = gpre.astype(BF16)
        for i in range(8):
            cols = pl.ds(i * PART, PART)
            pall[u, i // 2, i % 2] = jnp.dot(gpre_bf, up[:, cols], preferred_element_type=F32).astype(BF16)
        p_copy(u).start()
        hid_t[:, pl.ds(u * PAIR, PAIR)] = hidden.T.astype(BF16)
        gpre_t[:, pl.ds(u * PAIR, PAIR)] = gpre.T.astype(BF16)

    halves = (pl.ds(0, SLOT), pl.ds(SLOT, SLOT))
    far_copy = lambda u, k: remote(
        q.at[u, yof(2), halves[k]], fb.at[k, u], rys, ryr.at[u, k], (dp, exof(1 - 2 * k))
    )
    near_copy = lambda u, k: remote(
        q.at[u, yof(1 - 2 * k), halves[1 - k]], db.at[k, u], rys, ryr.at[u, 2 + k], (dp, exof(1 - 2 * k))
    )
    sum_copy = lambda u, k: remote(
        cs.at[k, u], cr.at[k, u], rys, ryr.at[u, 4 + k], (dp, exof(1 - 2 * k))
    )

    def core_sum(u):
        p_copy(u).wait_recv()
        for dy in (2, 1, -1, 0):
            at = yof(dy)
            q[u, at] = (pall[u, at, core].astype(F32) + pr[u, at].astype(F32)).astype(BF16)
            if dy == 2:
                far_copy(u, 0).start()
                far_copy(u, 1).start()
            elif dy == 1:
                near_copy(u, 0).start()
            elif dy == -1:
                near_copy(u, 1).start()

    def pair_sum(u):
        for k in (0, 1):
            far_copy(u, k).wait_recv()
            own = q[u, yof(1 - 2 * k), halves[k]].astype(F32)
            cs[k, u] = (fb[k, u].astype(F32) + own).astype(BF16)
            sum_copy(u, k).start()

    rx_copy = lambda u, dx: remote(
        ts.at[u, dx - 1], u_buf.at[pl.ds(2 * u, 2), dx], rxs, rxr.at[u, dx - 1], (xz(-dx, 0), ex)
    )

    def full_sum(u):
        for k in (0, 1):
            near_copy(u, k).wait_recv()
            sum_copy(u, k).wait_recv()
        for k in (0, 1):
            own = q[u, y, halves[k]].astype(F32)
            total = own + db[1 - k, u].astype(F32) + cr[k, u].astype(F32)
            total = total.astype(BF16).reshape(NX, CAP, PART)
            u_buf[2 * u + k, 0] = total[0]
            for dx in range(1, NX):
                ts[u, dx - 1, k] = total[dx]
        for dx in range(1, NX):
            rx_copy(u, dx).start()

    def rz_copy(r):
        step = -(r + 1) // 2 if r % 2 else r // 2
        return remote(u_buf.at[r], v_buf.at[r], rzs, rzr.at[r], (xz(0, step), ex))

    def give_back(u):
        for dx in range(1, NX):
            rx_copy(u, dx).wait_recv()
        if u == 0:
            v_buf[0] = u_buf[0]
        else:
            rz_copy(2 * u).start()
        rz_copy(2 * u + 1).start()

    tn = (((1,), (0,)), ((), ()))

    def weight_grads(e):
        cols = pl.ds(e * PART, PART)
        for first, left, out in ((0, gpre_t, gup), (PART, hid_t, gdown)):
            right = rows[e, :, :, :, pl.ds(first, PART)].reshape(ROWS, PART)
            out[:, cols] = lax.dot_general(
                left[pl.ds(0, HID)], right, tn, preferred_element_type=F32
            ).astype(BF16)

    def own_places(_):
        meta = zbuf[0, pl.ds(TOK, META)].astype(F32)
        line = lax.broadcasted_iota(jnp.int32, (4 * NZ, TOK), 0)
        r, dx = line // NX, line & (NX - 1)
        away = jnp.where((r & 1) == 0, r // 2, NZ - (r + 1) // 2)
        ids = ((x + dx) & (NX - 1)) * NZ + ((z + NZ - away) & (NZ - 1))
        slot, _ = slots_of(meta, ids.astype(F32), tri[...])
        for u in range(UNITS):
            hot = [place_rows(slot, None, NX * (2 * u + i))[0] for i in (0, 1)]
            own_hot[u] = jnp.concatenate(hot, axis=0).T.astype(BF16)

    steps = dict(
        Z=arrive, A=pick, B=spread, C=pass_on, D=far_side, F=compute, G=core_sum, H=pair_sum, I=full_sum,
        J=give_back, W=weight_grads, O=own_places,
    )
    first_matmul = next(i for i, (name, _) in enumerate(ORDER) if name == "F")
    for i, (name, which) in enumerate(ORDER):
        if i == first_matmul:
            load_up.wait()
            load_down.wait()
        steps[name](which)

    def all_sent(like, send, recv):
        remote(like, like, send, recv, (dp, partner)).wait_send()

    all_sent(zbuf.at[pl.ds(1, NZ - 1)], zs, zr.at[1, 0])
    all_sent(xs, xsem, xrem.at[0, 0])
    all_sent(rows.at[pl.ds(0, 2)], y1s, y1r.at[0, 0])
    all_sent(rows.at[pl.ds(0, 1)], y2s, y2r.at[0, 0])
    all_sent(rows.at[pl.ds(0, 4)], cos, cor.at[0, 0])
    all_sent(pr, rps, rpr.at[0])
    all_sent(q.at[pl.ds(0, 6)], rys, ryr.at[0, 0])
    all_sent(ts, rxs, rxr.at[0, 0])

    total = jnp.zeros((TOK, PART), F32)
    for u in [which for name, which in ORDER if name == "J"]:
        if u:
            rz_copy(2 * u).wait_recv()
        rz_copy(2 * u + 1).wait_recv()
        total = total + jnp.dot(
            own_hot[u], v_buf[pl.ds(2 * u, 2)].reshape(TOK, PART), preferred_element_type=F32
        )
    gtok[...] = total
    all_sent(u_buf.at[pl.ds(1, NZ - 1)], rzs, rzr.at[1])


def put_out(gtok, gup, gdown, gtok_out, gup_out, gdown_out, sem):
    copies = [
        pltpu.make_async_copy(src, dst, sem.at[i])
        for i, (src, dst) in enumerate(((gup, gup_out), (gdown, gdown_out), (gtok, gtok_out)))
    ]
    for copy in copies:
        copy.start()
    for copy in copies:
        copy.wait()


def local(tokens, arms, arm_bias, routes, gates, up_weight, down_weight, cotangent):
    hbm = pl.BlockSpec(memory_space=pltpu.HBM)
    vmem = pl.BlockSpec(memory_space=pltpu.VMEM)
    dma = pltpu.SemaphoreType.DMA
    pair = lambda *shape: [dma, dma(shape)]
    out_shape = (
        jax.ShapeDtypeStruct((TOK, PART), F32),
        jax.ShapeDtypeStruct((HID, WIDTH), BF16),
        jax.ShapeDtypeStruct((HID, WIDTH), BF16),
    )
    operands = (
        tokens, arms.reshape(1, TOK), arm_bias, routes.T, gates.T, up_weight[0], down_weight[0], cotangent
    )
    results = pl.pallas_call(
        kernel,
        out_shape=out_shape,
        in_specs=[hbm] * 8,
        out_specs=(vmem, vmem, vmem),
        scratch_shapes=[
            pltpu.VMEM((TOK, PART), BF16),
            pltpu.VMEM((1, TOK), jnp.int32),
            pltpu.VMEM(arm_bias.shape, BF16),
            pltpu.VMEM((TOPK, TOK), jnp.int32),
            pltpu.VMEM((TOPK, TOK), jnp.int32),
            pltpu.VMEM((NZ, 2 * TOK + META, PART), BF16),
            pltpu.VMEM((NX - 1, NZ, CAP, 2 * PART), BF16),
            pltpu.VMEM((8, NZ, NX, CAP, 2 * PART), BF16),
            pltpu.VMEM((HPAD, WIDTH), BF16),
            pltpu.VMEM((HPAD, WIDTH), BF16),
            pltpu.VMEM((HPAD, ROWS), BF16),
            pltpu.VMEM((HPAD, ROWS), BF16),
            pltpu.VMEM((UNITS, NY, 2, PAIR, PART), BF16),
            pltpu.VMEM((UNITS, NY, PAIR, PART), BF16),
            pltpu.VMEM((UNITS, NY, PAIR, PART), BF16),
            pltpu.VMEM((2, UNITS, SLOT, PART), BF16),
            pltpu.VMEM((2, UNITS, SLOT, PART), BF16),
            pltpu.VMEM((2, UNITS, SLOT, PART), BF16),
            pltpu.VMEM((2, UNITS, SLOT, PART), BF16),
            pltpu.VMEM((UNITS, NX - 1, 2, CAP, PART), BF16),
            pltpu.VMEM((NZ, NX, CAP, PART), BF16),
            pltpu.VMEM((NZ, NX, CAP, PART), BF16),
            pltpu.VMEM((TOK, TOK), BF16),
            pltpu.VMEM((UNITS, TOK, TOK), BF16),
            dma((8,)),
            *pair(NZ, 2),
            *pair(NZ, NX - 1),
            *pair(NZ, 2),
            *pair(NZ, 2),
            *pair(NZ, 4),
            *pair(UNITS),
            *pair(UNITS, 6),
            *pair(UNITS, NX - 1),
            *pair(NZ),
        ],
        compiler_params=pltpu.CompilerParams(
            collective_id=0, has_side_effects=True, vmem_limit_bytes=36 * 1024 * 1024
        ),
        name="expert_backward",
    )(*(pltpu.with_memory_space_constraint(a, pltpu.HBM) for a in operands))
    grad_tokens, grad_up, grad_down = pl.pallas_call(
        put_out,
        out_shape=out_shape,
        in_specs=[vmem] * 3,
        out_specs=(hbm, hbm, hbm),
        scratch_shapes=[dma((3,))],
        compiler_params=pltpu.CompilerParams(vmem_limit_bytes=4 * 1024 * 1024),
        name="put_out",
    )(*results)
    return grad_tokens, grad_up[None], grad_down[None]


def solution(mesh):
    in_specs = (
        P("dp", None),
        P("dp"),
        P(),
        P("dp", None),
        P("dp", None),
        P("dp", "expert", None),
        P("dp", "expert", None),
        P("dp", None),
    )
    out_specs = (P("dp", "expert"), P("dp", "expert", None), P("dp", "expert", None))
    return jax.shard_map(local, mesh=mesh, in_specs=in_specs, out_specs=out_specs, check_vma=False)
```

```python
import jax
import jax.numpy as jnp
from jax import lax
from jax.experimental import pallas as pl
from jax.experimental.pallas import tpu as pltpu
from jax.sharding import PartitionSpec as P

MESH = pl.DeviceIdType.MESH
F32, BF16 = jnp.float32, jnp.bfloat16

TOK = 128
CAP = 16
PART = 256
HID = 176
HPAD = 256
PAIR = 128
NX, NY, NZ = 4, 4, 16
META = 16
TOPK = 6
UNITS = 8
SLOT = 64
ROWS = 1024
WIDTH = 2048

ORDER = (
    ("A", 0), ("Z", 4), ("Z", 2), ("Z", 3), ("Z", 5), ("A", 1), ("B", 0), ("Z", 6), ("Z", 8), ("A", 2),
    ("Z", 9), ("A", 4), ("Z", 7), ("A", 3), ("B", 1), ("Z", 12), ("Z", 10), ("B", 2), ("Z", 13), ("Z", 11),
    ("A", 6), ("B", 4), ("Z", 16), ("C", 2), ("Z", 17), ("Z", 14), ("B", 3), ("Z", 15), ("A", 8), ("B", 6),
    ("C", 3), ("Z", 21), ("Z", 20), ("Z", 18), ("Z", 19), ("A", 9), ("A", 10), ("A", 7), ("B", 8), ("C", 1),
    ("Z", 25), ("C", 6), ("B", 9), ("Z", 24), ("Z", 22), ("A", 5), ("D", 3), ("Z", 23), ("A", 11), ("A", 12),
    ("C", 0), ("C", 8), ("D", 6), ("B", 7), ("Z", 27), ("C", 9), ("D", 2), ("B", 11), ("D", 8), ("O", 0),
    ("Z", 26), ("B", 12), ("D", 9), ("A", 13), ("Z", 31), ("B", 10), ("C", 11), ("B", 5), ("F", 1), ("C", 12),
    ("F", 4), ("Z", 29), ("B", 13), ("Z", 28), ("C", 10), ("Z", 30), ("C", 5), ("A", 15), ("G", 4), ("A", 14),
    ("G", 1), ("D", 12), ("D", 10), ("C", 13), ("D", 11), ("H", 4), ("D", 5), ("B", 15), ("C", 4), ("D", 1),
    ("F", 5), ("D", 13), ("B", 14), ("G", 5), ("C", 15), ("I", 4), ("H", 1), ("F", 6), ("C", 14), ("D", 4),
    ("D", 0), ("C", 7), ("H", 5), ("G", 6), ("D", 15), ("D", 14), ("I", 1), ("J", 4), ("F", 0), ("D", 7),
    ("I", 5), ("H", 6), ("F", 7), ("J", 1), ("I", 6), ("G", 7), ("J", 5), ("G", 0), ("F", 3), ("H", 7),
    ("F", 2), ("J", 6), ("G", 3), ("I", 7), ("G", 2), ("H", 3), ("J", 7), ("W", 3), ("H", 0), ("H", 2),
    ("I", 3), ("I", 0), ("I", 2), ("W", 2), ("W", 7), ("J", 3), ("J", 2), ("W", 6), ("W", 0), ("J", 0),
    ("W", 1), ("W", 4), ("W", 5),
)


def place_rows(slot, gate, first):
    index = lax.broadcasted_iota(jnp.int32, (CAP, TOK), 0).astype(F32)
    hot, weighted = [], []
    for i in range(NX):
        here = jnp.broadcast_to(slot[first + i : first + i + 1], (CAP, TOK)) == index
        hot.append(jnp.where(here, 1.0, 0.0))
        if gate is not None:
            weight = jnp.broadcast_to(gate[first + i : first + i + 1], (CAP, TOK))
            weighted.append(jnp.where(here, weight, 0.0))
    hot = jnp.concatenate(hot, axis=0)
    return hot, (jnp.concatenate(weighted, axis=0) if weighted else None)


def slots_of(meta, ids, earlier):
    hits = jnp.zeros(ids.shape, F32)
    gate = jnp.zeros(ids.shape, F32)
    for k in range(TOPK):
        same = jnp.broadcast_to(meta[k : k + 1, :TOK], ids.shape) == ids
        hits = hits + jnp.where(same, 1.0, 0.0)
        gate = gate + jnp.where(same, jnp.broadcast_to(meta[k : k + 1, TOK:], ids.shape), 0.0)
    rank = jnp.dot(hits.astype(BF16), earlier, preferred_element_type=F32)
    return jnp.where(hits > 0.5, rank, -1.0), gate


def kernel(
    tokens, arms_in, bias_in, routes_in, gates_in, up_in, down_in, cot,
    gtok, gup, gdown,
    tok, arms, bias, routes, gates, zbuf, xs, rows, up, down, hid_t, gpre_t, pall, pr, q, fb, db, cs, cr, ts,
    u_buf, v_buf, tri, own_hot,
    in_sem, zs, zr, xsem, xrem, y1s, y1r, y2s, y2r, cos, cor, rps, rpr, rys, ryr, rxs, rxr, rzs, rzr,
):
    dp, ex = lax.axis_index("dp"), lax.axis_index("expert")
    x, z = dp // NZ, lax.rem(dp, NZ)
    y, core = ex // 2, lax.rem(ex, 2)
    xz = lambda dx, dz: lax.rem(x + dx + NX, NX) * NZ + lax.rem(z + dz + NZ, NZ)
    yof = lambda dy: lax.rem(y + dy + NY, NY)
    exof = lambda dy: yof(dy) * 2 + core
    partner = y * 2 + (1 - core)

    def remote(src, dst, send, recv, to):
        return pltpu.make_async_remote_copy(
            src_ref=src, dst_ref=dst, send_sem=send, recv_sem=recv, device_id=to, device_id_type=MESH
        )

    lanes = pl.ds(pl.multiple_of(ex * PART, PART), PART)
    local_copy = lambda src, dst, i: pltpu.make_async_copy(src, dst, in_sem.at[i])
    load_tok = local_copy(tokens.at[:, lanes], tok, 0)
    load_cot = local_copy(cot.at[:, lanes], zbuf.at[0, pl.ds(TOK + META, TOK)], 1)
    load_up = local_copy(up_in, up.at[pl.ds(0, HID)], 2)
    load_down = local_copy(down_in, down.at[pl.ds(0, HID)], 3)
    load_small = [
        local_copy(arms_in, arms, 4), local_copy(bias_in, bias, 5),
        local_copy(routes_in, routes, 6), local_copy(gates_in, gates, 7),
    ]
    for load in (*load_small, load_tok, load_cot):
        load.start()

    barrier = pltpu.get_barrier_semaphore()
    peers = [(xz(d, 0), ex) for d in (1, 2, 3)]
    peers += [(xz(0, 1), ex), (xz(0, -1), ex), (dp, exof(1)), (dp, exof(-1)), (dp, partner)]
    for to in peers:
        pl.semaphore_signal(barrier, inc=1, device_id=to, device_id_type=MESH)

    tri[...] = jnp.where(
        lax.broadcasted_iota(jnp.int32, (TOK, TOK), 0) < lax.broadcasted_iota(jnp.int32, (TOK, TOK), 1), 1.0, 0.0
    ).astype(BF16)
    for load in load_small:
        load.wait()
    arm_row = jnp.broadcast_to(arms[...], (TOK, TOK))
    arm_hot = jnp.where(arm_row == lax.broadcasted_iota(jnp.int32, (TOK, TOK), 0), 1.0, 0.0).T
    own_bias = bias[:, lanes].astype(F32)
    added = jnp.zeros((TOK, PART), F32)
    for a in range(own_bias.shape[0]):
        added = added + arm_hot[:, a : a + 1] * own_bias[a : a + 1]
    line = lax.broadcasted_iota(jnp.int32, (META, TOK), 0)
    for at, table in ((0, routes), (TOK, gates)):
        packed = jnp.zeros((META, TOK), F32)
        for k in range(TOPK):
            packed = jnp.where(line == k, jnp.broadcast_to(table[k : k + 1].astype(F32), (META, TOK)), packed)
        zbuf[0, pl.ds(TOK, META), pl.ds(at, TOK)] = packed.astype(BF16)
    load_tok.wait()
    zbuf[0, pl.ds(0, TOK)] = (tok[...].astype(F32) + added).astype(BF16)
    load_cot.wait()
    pl.semaphore_wait(barrier, len(peers))

    pieces = ((0, TOK + META), (TOK + META, TOK))

    def z_copy(to_slot, piece):
        at = pl.ds(*pieces[piece])
        step = 1 if to_slot % 2 else -1
        return remote(
            zbuf.at[max(to_slot - 2, 0), at], zbuf.at[to_slot, at],
            zs, zr.at[to_slot, piece], (xz(0, step), ex),
        )

    for piece in range(len(pieces)):
        z_copy(1, piece).start()
        z_copy(2, piece).start()
    load_up.start()
    load_down.start()
    up[pl.ds(HID, HPAD - HID)] = jnp.zeros((HPAD - HID, WIDTH), BF16)
    down[pl.ds(HID, HPAD - HID)] = jnp.zeros((HPAD - HID, WIDTH), BF16)

    x_copy = lambda r, dx: remote(
        xs.at[dx - 1, r], rows.at[ex, r, dx], xsem, xrem.at[r, dx - 1], (xz(dx, 0), ex)
    )
    y1_copy = lambda r, k: remote(
        rows.at[ex, r], rows.at[ex, r], y1s, y1r.at[r, k], (dp, exof(1 - 2 * k))
    )

    def y2_copy(r, k):
        part = rows.at[exof(2 * k - 1), r, pl.ds(2 * k, 2)]
        return remote(part, part, y2s, y2r.at[r, k], (dp, exof(1 - 2 * k)))

    def core_copy(r, k):
        part = rows.at[exof((0, -1, 1, 2)[k]), r]
        return remote(part, part, cos, cor.at[r, k], (dp, partner))

    turn = lax.broadcasted_iota(jnp.int32, (CAP, TOK), 0)
    here = (((x + turn) & (NX - 1)) * NZ + z).astype(F32)

    def arrive(which):
        r, piece = which // 2, which % 2
        z_copy(r, piece).wait_recv()
        if r + 2 < NZ:
            z_copy(r + 2, piece).start()

    def pick(r):
        meta = zbuf[r, pl.ds(TOK, META)].astype(F32)
        slot, gate = slots_of(meta, here, tri[...])
        hot, weighted = place_rows(slot, gate * (1.0 / 64.0), 0)
        for first, chosen, base in ((0, hot, 0), (PART, weighted, TOK + META)):
            picked = jnp.dot(
                chosen.astype(BF16), zbuf[r, pl.ds(base, TOK)], preferred_element_type=F32
            ).astype(BF16)
            rows[ex, r, 0, :, pl.ds(first, PART)] = picked[:CAP]
            for dx in range(1, NX):
                xs[dx - 1, r, :, pl.ds(first, PART)] = picked[dx * CAP : (dx + 1) * CAP]
        for dx in range(1, NX):
            x_copy(r, dx).start()

    def spread(r):
        for dx in range(1, NX):
            x_copy(r, dx).wait_recv()
        y1_copy(r, 0).start()
        y1_copy(r, 1).start()
        core_copy(r, 0).start()

    def pass_on(r):
        for k in (0, 1):
            y1_copy(r, k).wait_recv()
            y2_copy(r, k).start()
            core_copy(r, 1 + k).start()

    def far_side(r):
        for k in (0, 1):
            y2_copy(r, k).wait_recv()
        core_copy(r, 3).start()

    p_copy = lambda u: remote(pall.at[u, :, 1 - core], pr.at[u], rps, rpr.at[u], (dp, partner))

    def compute(u):
        for r in (2 * u, 2 * u + 1):
            for k in range(4):
                core_copy(r, k).wait_recv()
        pre = jnp.zeros((PAIR, HPAD), F32)
        back = jnp.zeros((PAIR, HPAD), F32)
        nt = (((1,), (1,)), ((), ()))
        for i in range(8):
            block = rows[i, pl.ds(2 * u, 2)].reshape(PAIR, 2 * PART)
            cols = pl.ds(i * PART, PART)
            pre = pre + lax.dot_general(block[:, :PART], up[:, cols], nt, preferred_element_type=F32)
            back = back + lax.dot_general(block[:, PART:], down[:, cols], nt, preferred_element_type=F32)
        sig = 1.0 / (1.0 + jnp.exp(-pre))
        hidden = pre * sig
        gpre = back * sig * (1.0 + pre * (1.0 - sig))
        gpre_bf = gpre.astype(BF16)
        for i in range(8):
            cols = pl.ds(i * PART, PART)
            pall[u, i // 2, i % 2] = jnp.dot(gpre_bf, up[:, cols], preferred_element_type=F32).astype(BF16)
        p_copy(u).start()
        hid_t[:, pl.ds(u * PAIR, PAIR)] = hidden.T.astype(BF16)
        gpre_t[:, pl.ds(u * PAIR, PAIR)] = gpre.T.astype(BF16)

    halves = (pl.ds(0, SLOT), pl.ds(SLOT, SLOT))
    far_copy = lambda u, k: remote(
        q.at[u, yof(2), halves[k]], fb.at[k, u], rys, ryr.at[u, k], (dp, exof(1 - 2 * k))
    )
    near_copy = lambda u, k: remote(
        q.at[u, yof(1 - 2 * k), halves[1 - k]], db.at[k, u], rys, ryr.at[u, 2 + k], (dp, exof(1 - 2 * k))
    )
    sum_copy = lambda u, k: remote(
        cs.at[k, u], cr.at[k, u], rys, ryr.at[u, 4 + k], (dp, exof(1 - 2 * k))
    )

    def core_sum(u):
        p_copy(u).wait_recv()
        for dy in (2, 1, -1, 0):
            at = yof(dy)
            q[u, at] = (pall[u, at, core].astype(F32) + pr[u, at].astype(F32)).astype(BF16)
            if dy == 2:
                far_copy(u, 0).start()
                far_copy(u, 1).start()
            elif dy == 1:
                near_copy(u, 0).start()
            elif dy == -1:
                near_copy(u, 1).start()

    def pair_sum(u):
        for k in (0, 1):
            far_copy(u, k).wait_recv()
            own = q[u, yof(1 - 2 * k), halves[k]].astype(F32)
            cs[k, u] = (fb[k, u].astype(F32) + own).astype(BF16)
            sum_copy(u, k).start()

    rx_copy = lambda u, dx: remote(
        ts.at[u, dx - 1], u_buf.at[pl.ds(2 * u, 2), dx], rxs, rxr.at[u, dx - 1], (xz(-dx, 0), ex)
    )

    def full_sum(u):
        for k in (0, 1):
            near_copy(u, k).wait_recv()
            sum_copy(u, k).wait_recv()
        for k in (0, 1):
            own = q[u, y, halves[k]].astype(F32)
            total = own + db[1 - k, u].astype(F32) + cr[k, u].astype(F32)
            total = total.astype(BF16).reshape(NX, CAP, PART)
            u_buf[2 * u + k, 0] = total[0]
            for dx in range(1, NX):
                ts[u, dx - 1, k] = total[dx]
        for dx in range(1, NX):
            rx_copy(u, dx).start()

    def rz_copy(r):
        step = -(r + 1) // 2 if r % 2 else r // 2
        return remote(u_buf.at[r], v_buf.at[r], rzs, rzr.at[r], (xz(0, step), ex))

    def give_back(u):
        for dx in range(1, NX):
            rx_copy(u, dx).wait_recv()
        if u == 0:
            v_buf[0] = u_buf[0]
        else:
            rz_copy(2 * u).start()
        rz_copy(2 * u + 1).start()

    tn = (((1,), (0,)), ((), ()))

    def weight_grads(e):
        cols = pl.ds(e * PART, PART)
        for first, left, out in ((0, gpre_t, gup), (PART, hid_t, gdown)):
            right = rows[e, :, :, :, pl.ds(first, PART)].reshape(ROWS, PART)
            out[:, cols] = lax.dot_general(
                left[pl.ds(0, HID)], right, tn, preferred_element_type=F32
            ).astype(BF16)

    def own_places(_):
        meta = zbuf[0, pl.ds(TOK, META)].astype(F32)
        line = lax.broadcasted_iota(jnp.int32, (4 * NZ, TOK), 0)
        r, dx = line // NX, line & (NX - 1)
        away = jnp.where((r & 1) == 0, r // 2, NZ - (r + 1) // 2)
        ids = ((x + dx) & (NX - 1)) * NZ + ((z + NZ - away) & (NZ - 1))
        slot, _ = slots_of(meta, ids.astype(F32), tri[...])
        for u in range(UNITS):
            hot = [place_rows(slot, None, NX * (2 * u + i))[0] for i in (0, 1)]
            own_hot[u] = jnp.concatenate(hot, axis=0).T.astype(BF16)

    steps = dict(
        Z=arrive, A=pick, B=spread, C=pass_on, D=far_side, F=compute, G=core_sum, H=pair_sum, I=full_sum,
        J=give_back, W=weight_grads, O=own_places,
    )
    first_matmul = next(i for i, (name, _) in enumerate(ORDER) if name == "F")
    for i, (name, which) in enumerate(ORDER):
        if i == first_matmul:
            load_up.wait()
            load_down.wait()
        steps[name](which)

    def all_sent(like, send, recv):
        remote(like, like, send, recv, (dp, partner)).wait_send()

    all_sent(zbuf.at[pl.ds(1, NZ - 1)], zs, zr.at[1, 0])
    all_sent(xs, xsem, xrem.at[0, 0])
    all_sent(rows.at[pl.ds(0, 2)], y1s, y1r.at[0, 0])
    all_sent(rows.at[pl.ds(0, 1)], y2s, y2r.at[0, 0])
    all_sent(rows.at[pl.ds(0, 4)], cos, cor.at[0, 0])
    all_sent(pr, rps, rpr.at[0])
    all_sent(q.at[pl.ds(0, 6)], rys, ryr.at[0, 0])
    all_sent(ts, rxs, rxr.at[0, 0])

    total = jnp.zeros((TOK, PART), F32)
    for u in [which for name, which in ORDER if name == "J"]:
        if u:
            rz_copy(2 * u).wait_recv()
        rz_copy(2 * u + 1).wait_recv()
        total = total + jnp.dot(
            own_hot[u], v_buf[pl.ds(2 * u, 2)].reshape(TOK, PART), preferred_element_type=F32
        )
    gtok[...] = total
    all_sent(u_buf.at[pl.ds(1, NZ - 1)], rzs, rzr.at[1])


def put_out(gtok, gup, gdown, gtok_out, gup_out, gdown_out, sem):
    copies = [
        pltpu.make_async_copy(src, dst, sem.at[i])
        for i, (src, dst) in enumerate(((gup, gup_out), (gdown, gdown_out), (gtok, gtok_out)))
    ]
    for copy in copies:
        copy.start()
    for copy in copies:
        copy.wait()


def local(tokens, arms, arm_bias, routes, gates, up_weight, down_weight, cotangent):
    hbm = pl.BlockSpec(memory_space=pltpu.HBM)
    vmem = pl.BlockSpec(memory_space=pltpu.VMEM)
    dma = pltpu.SemaphoreType.DMA
    pair = lambda *shape: [dma, dma(shape)]
    out_shape = (
        jax.ShapeDtypeStruct((TOK, PART), F32),
        jax.ShapeDtypeStruct((HID, WIDTH), BF16),
        jax.ShapeDtypeStruct((HID, WIDTH), BF16),
    )
    operands = (
        tokens, arms.reshape(1, TOK), arm_bias, routes.T, gates.T, up_weight[0], down_weight[0], cotangent
    )
    results = pl.pallas_call(
        kernel,
        out_shape=out_shape,
        in_specs=[hbm] * 8,
        out_specs=(vmem, vmem, vmem),
        scratch_shapes=[
            pltpu.VMEM((TOK, PART), BF16),
            pltpu.VMEM((1, TOK), jnp.int32),
            pltpu.VMEM(arm_bias.shape, BF16),
            pltpu.VMEM((TOPK, TOK), jnp.int32),
            pltpu.VMEM((TOPK, TOK), jnp.int32),
            pltpu.VMEM((NZ, 2 * TOK + META, PART), BF16),
            pltpu.VMEM((NX - 1, NZ, CAP, 2 * PART), BF16),
            pltpu.VMEM((8, NZ, NX, CAP, 2 * PART), BF16),
            pltpu.VMEM((HPAD, WIDTH), BF16),
            pltpu.VMEM((HPAD, WIDTH), BF16),
            pltpu.VMEM((HPAD, ROWS), BF16),
            pltpu.VMEM((HPAD, ROWS), BF16),
            pltpu.VMEM((UNITS, NY, 2, PAIR, PART), BF16),
            pltpu.VMEM((UNITS, NY, PAIR, PART), BF16),
            pltpu.VMEM((UNITS, NY, PAIR, PART), BF16),
            pltpu.VMEM((2, UNITS, SLOT, PART), BF16),
            pltpu.VMEM((2, UNITS, SLOT, PART), BF16),
            pltpu.VMEM((2, UNITS, SLOT, PART), BF16),
            pltpu.VMEM((2, UNITS, SLOT, PART), BF16),
            pltpu.VMEM((UNITS, NX - 1, 2, CAP, PART), BF16),
            pltpu.VMEM((NZ, NX, CAP, PART), BF16),
            pltpu.VMEM((NZ, NX, CAP, PART), BF16),
            pltpu.VMEM((TOK, TOK), BF16),
            pltpu.VMEM((UNITS, TOK, TOK), BF16),
            dma((8,)),
            *pair(NZ, 2),
            *pair(NZ, NX - 1),
            *pair(NZ, 2),
            *pair(NZ, 2),
            *pair(NZ, 4),
            *pair(UNITS),
            *pair(UNITS, 6),
            *pair(UNITS, NX - 1),
            *pair(NZ),
        ],
        compiler_params=pltpu.CompilerParams(
            collective_id=0, has_side_effects=True, vmem_limit_bytes=36 * 1024 * 1024
        ),
        name="expert_backward",
    )(*(pltpu.with_memory_space_constraint(a, pltpu.HBM) for a in operands))
    grad_tokens, grad_up, grad_down = pl.pallas_call(
        put_out,
        out_shape=out_shape,
        in_specs=[vmem] * 3,
        out_specs=(hbm, hbm, hbm),
        scratch_shapes=[dma((3,))],
        compiler_params=pltpu.CompilerParams(vmem_limit_bytes=4 * 1024 * 1024),
        name="put_out",
    )(*results)
    return grad_tokens, grad_up[None], grad_down[None]


def solution(mesh):
    in_specs = (
        P("dp", None),
        P("dp"),
        P(),
        P("dp", None),
        P("dp", None),
        P("dp", "expert", None),
        P("dp", "expert", None),
        P("dp", None),
    )
    out_specs = (P("dp", "expert"), P("dp", "expert", None), P("dp", "expert", None))
    return jax.shard_map(local, mesh=mesh, in_specs=in_specs, out_specs=out_specs, check_vma=False)
```
